32 devices in a mesh: member: 2 (over y), tx: 4 (over z), ty: 4 (over x, core).
Axes of the slice: x: 2, y: 2, z: 4, core: 2. Of those that a mesh axis runs over, the one named last changes fastest.
Arguments:
- tracers: float32 [80, 3, 128, 512], P('member', None, 'tx', 'ty'), parts along dimension 0, may hold values from 0.05 to 2
- velocity: float32 [2, 3, 128, 512], P(None, None, 'tx', 'ty'), may hold values from -0.4 to 0.4
- land_mask: int32 [3, 128, 512], P(None, 'tx', 'ty'), may hold values 0 or 1
- sunlight: float32 [128, 512], P('tx', 'ty'), may hold values from 0.3 to 3
- growth_max: float32 [52], P('member'), parts along dimension 0, may hold values from 0.2 to 1.5
- half_sat: float32 [8, 26], P('member'), parts along dimension 0, may hold values from 0.05 to 1
- light_half: float32 [52], P('member'), parts along dimension 0, may hold values from 0.1 to 1
- graze_max: float32 [20], P('member'), parts along dimension 0, may hold values from 0.2 to 1.5
- graze_half: float32 [20], P('member'), parts along dimension 0, may hold values from 0.2 to 2
- palatable: int32 [20, 26], P('member'), parts along dimension 0, may hold values 0 or 1
- stoichiometry: float32 [4], replicated, may hold values from 0.05 to 1
Outputs:
- updated: float32 [80, 3, 128, 512], P('member', None, 'tx', 'ty'), parts along dimension 0
The draws below stay inside these ranges and needn't reach their ends.
There are 2 independent parts, one for each index of `member`. The reference program is written for one: setup_inputs(seed, part) draws one part's arguments, and reference() takes and returns one part's arrays. A program takes and returns all parts, laid end to end along the dimension named above; an argument that names none is the same for every part. Nothing has to cross between parts.
All inputs are finite; a program needn't handle non-finite values. No bound on the sum of `land_mask` on one device may be relied on, other than what follows from the above.
Results may differ from the reference program's by a relative error of at most 0.000064.
Values sent between devices are 32-bit elements; how exact they have to be, the bound alone decides.
No kernel may reach another device: no remote copies, remote signals or barrier semaphores. Data moves between devices by JAX's collectives and lax.ppermute only.
A program may use at most 64 MiB of HBM per device.

```python
import math
import jax
import jax.numpy as jnp
from jax import lax

NNUT = 4
NPHY = 26
NZOO = 10
NR = 3
NTR = 40
NX = 128
NY = 512


def with_ends(entries, rng, least, high):
    dims = entries.shape
    spot = [jax.random.randint(jax.random.fold_in(rng, axis), (), 0, dims[axis]) for axis in range(len(dims))]
    entries = entries.at[tuple(spot)].set(least)
    longest = dims.index(max(dims))
    spot[longest] = (spot[longest] + 1) % dims[longest]
    return entries.at[tuple(spot)].set(high)


def block_scale(own_key, dims, cuts, low, largest):
    loudness = 1.0
    for dim, blocks in cuts:
        steps = jax.random.uniform(jax.random.fold_in(jax.random.fold_in(own_key, 6), dim), (blocks,), jnp.float32, low / len(cuts), largest / len(cuts))
        loudness = loudness * jnp.repeat(jnp.exp(steps), dims[dim] // blocks).reshape((-1,) + (1,) * (len(dims) - 1 - dim))
    return loudness


def setup_inputs(seed: int = 0, part: int = 0) -> dict:
    keys = jax.random.split(jax.random.key(seed), 12)
    own_keys = jax.random.split(jax.random.fold_in(keys[11], part), 12)
    tracers = jnp.clip(jnp.exp(math.log(2.0) - 3.6888794 * jax.random.uniform(own_keys[0], (NTR, NR, NX, NY), jnp.float32) ** block_scale(own_keys[0], (NTR, NR, NX, NY), ((2, 4), (3, 4)), -0.2, 0.2)), 0.05, 2.0)
    velocity = jnp.clip(jax.random.uniform(keys[1], (2, NR, NX, NY), jnp.float32, -0.4, 0.4) * block_scale(keys[1], (2, NR, NX, NY), ((2, 4), (3, 4)), -0.4, 0.0), -0.4, 0.4)
    land_mask = with_ends((jax.random.randint(keys[2], (NR, NX, NY), 0, 5) < 4).astype(jnp.int32), jax.random.fold_in(keys[2], 1), 0, 1)
    sunlight = jnp.clip(jnp.exp(math.log(3.0) - 2.3025851 * jax.random.uniform(keys[3], (NX, NY), jnp.float32) ** block_scale(keys[3], (NX, NY), ((0, 4), (1, 4)), -0.2, 0.2)), 0.3, 3.0)
    growth_max = jnp.clip(jnp.exp(jax.random.uniform(own_keys[4], (NPHY,), jnp.float32, math.log(0.2), math.log(1.5))), 0.2, 1.5)
    half_sat = jnp.clip(jnp.exp(jax.random.uniform(own_keys[5], (NNUT, NPHY), jnp.float32, math.log(0.05), math.log(1.0))), 0.05, 1.0)
    light_half = jnp.clip(jnp.exp(jax.random.uniform(own_keys[6], (NPHY,), jnp.float32, math.log(0.1), math.log(1.0))), 0.1, 1.0)
    graze_max = jnp.clip(jnp.exp(jax.random.uniform(own_keys[7], (NZOO,), jnp.float32, math.log(0.2), math.log(1.5))), 0.2, 1.5)
    graze_half = jnp.clip(jnp.exp(jax.random.uniform(own_keys[8], (NZOO,), jnp.float32, math.log(0.2), math.log(2.0))), 0.2, 2.0)
    palatable = with_ends((jax.random.randint(own_keys[9], (NZOO, NPHY), 0, 2) < 1).astype(jnp.int32), jax.random.fold_in(own_keys[9], 1), 0, 1)
    stoichiometry = jnp.clip(jnp.exp(jax.random.uniform(keys[10], (NNUT,), jnp.float32, math.log(0.05), math.log(1.0))), 0.05, 1.0)
    return dict(tracers=tracers, velocity=velocity, land_mask=land_mask, sunlight=sunlight, growth_max=growth_max, half_sat=half_sat, light_half=light_half, graze_max=graze_max, graze_half=graze_half, palatable=palatable, stoichiometry=stoichiometry)


plankton_mortality = 0.05
grazer_mortality = 0.3
assimilation = 0.3
attenuation = 0.4


def window(values, offset, amount, axis_dim):
    return lax.slice_in_dim(values, offset, offset + amount, axis=axis_dim)


def advect(padded, courant, wet_mask, axis_dim, length):
    face_count = length + 1
    far_left = window(padded, 0, face_count, axis_dim)
    near_left = window(padded, 1, face_count, axis_dim)
    near_right = window(padded, 2, face_count, axis_dim)
    far_right = window(padded, 3, face_count, axis_dim)
    opened = window(wet_mask, 1, face_count, axis_dim) * window(wet_mask, 2, face_count, axis_dim)
    transport = window(courant, 2, face_count, axis_dim) * opened
    face_flux = transport * ((7.0 / 12.0) * (near_left + near_right) - (1.0 / 12.0) * (far_left + far_right))
    face_flux = face_flux + jnp.abs(transport) * (1.0 / 12.0) * (far_right - 3.0 * near_right + 3.0 * near_left - far_left)
    centre = window(padded, 2, length, axis_dim)
    outflow = window(face_flux, 1, length, axis_dim) - window(face_flux, 0, length, axis_dim)
    spread = window(transport, 1, length, axis_dim) - window(transport, 0, length, axis_dim)
    return centre - outflow + centre * spread


def ecology(concentration, irradiance, growth_max, half_sat, light_half, graze_max, graze_half, palatable, stoichiometry):
    nutrients = concentration[:NNUT]
    phytoplankton = concentration[NNUT:NNUT + NPHY]
    zooplankton = concentration[NNUT + NPHY:]
    saturation = nutrients[:, None, :] / (nutrients[:, None, :] + half_sat[:, :, None])
    nutrient_limit = jnp.min(saturation, axis=0)
    light_limit = irradiance[None, :] / (irradiance[None, :] + light_half[:, None])
    growth = growth_max[:, None] * nutrient_limit * light_limit * phytoplankton
    prey_weights = palatable.astype(jnp.float32)
    available = jnp.dot(prey_weights, phytoplankton, precision=lax.Precision.HIGHEST)
    grazing_rate = graze_max[:, None] * zooplankton / (graze_half[:, None] + available)
    grazed = phytoplankton * jnp.dot(prey_weights.T, grazing_rate, precision=lax.Precision.HIGHEST)
    ingested = grazing_rate * available
    plankton_loss = plankton_mortality * phytoplankton
    grazer_loss = grazer_mortality * zooplankton * zooplankton
    phyto_change = growth - grazed - plankton_loss
    grazer_change = assimilation * ingested - grazer_loss
    recycled = jnp.sum(plankton_loss, axis=0) + jnp.sum(grazer_loss, axis=0) + (1.0 - assimilation) * jnp.sum(ingested, axis=0) - jnp.sum(growth, axis=0)
    nutrient_change = stoichiometry[:, None] * recycled[None, :]
    return jnp.concatenate([nutrient_change, phyto_change, grazer_change], axis=0)


def reference(tracers, velocity, land_mask, sunlight, growth_max, half_sat, light_half, graze_max, graze_half, palatable, stoichiometry):
    def pad_along(values):
        return jnp.pad(values, ((0, 0), (0, 0), (2, 2), (0, 0)), mode="wrap")

    def pad_across(values):
        return jnp.pad(values, ((0, 0), (0, 0), (0, 0), (2, 2)))

    def one_layer(layer_index):
        concentration = lax.dynamic_slice_in_dim(tracers, layer_index, 1, 1)
        flow = lax.dynamic_slice_in_dim(velocity, layer_index, 1, 1)
        wet_mask = lax.dynamic_slice_in_dim(land_mask, layer_index, 1, 0).astype(jnp.float32)[None]
        after_along = advect(pad_along(concentration), pad_along(flow[0:1]), pad_along(wet_mask), 2, NX)
        advected = advect(pad_across(after_along), pad_across(flow[1:2]), pad_across(wet_mask), 3, NY)
        depth_factor = jnp.exp(-attenuation * (layer_index.astype(jnp.float32) + 0.5))
        irradiance = (sunlight * depth_factor).reshape(-1)
        tendency = ecology(concentration.reshape(NTR, -1), irradiance, growth_max, half_sat, light_half, graze_max, graze_half, palatable, stoichiometry)
        return advected + wet_mask * tendency.reshape(concentration.shape)

    layers = lax.map(one_layer, jnp.arange(NR, dtype=jnp.int32))
    return jnp.moveaxis(layers[:, :, 0], 0, 1)
```

```python
import functools

import jax
import jax.numpy as jnp
from jax import lax
from jax.experimental import pallas as pl
from jax.experimental.pallas import tpu as pltpu
from jax.sharding import PartitionSpec as P

NNUT = 4
NPHY = 26
PAD = 4

plankton_mortality = 0.05
grazer_mortality = 0.3
assimilation = 0.3
attenuation = 0.4

VMEM = pl.BlockSpec(memory_space=pltpu.VMEM)
SMEM = pl.BlockSpec(memory_space=pltpu.SMEM)
ANY = pl.BlockSpec(memory_space=pl.ANY)


def in_vmem(array):
    return pltpu.with_memory_space_constraint(array, pltpu.VMEM)


def call(kernel, outs, specs, scratch=(), flops=0, bytes_accessed=0, limit=8 << 20, **more):
    return pl.pallas_call(
        kernel,
        out_shape=outs,
        in_specs=specs,
        scratch_shapes=list(scratch),
        cost_estimate=pl.CostEstimate(flops=flops, bytes_accessed=bytes_accessed, transcendentals=0),
        compiler_params=pltpu.CompilerParams(vmem_limit_bytes=limit),
        **more,
    )


def pack_rows(tracers, velocity, mask, first, last, edge, sems):
    count, length = tracers.shape[0], tracers.shape[1]
    levels = mask.shape[0]
    groups = first.shape[0]
    copies = []
    for side, (out, start) in enumerate(((first, 0), (last, length - 2))):
        rows = pl.ds(start, 2)
        copies += [
            pltpu.make_async_copy(tracers.at[:, rows], out.at[pl.ds(PAD, count)], sems.at[side, 0]),
            pltpu.make_async_copy(
                velocity.at[0, :, rows], out.at[pl.ds(PAD + count, levels)], sems.at[side, 1]
            ),
            pltpu.make_async_copy(mask.at[:, rows], edge.at[side], sems.at[side, 2]),
        ]
    for copy in copies:
        copy.start()
    for out in (first, last):
        out[0:PAD] = jnp.zeros((PAD,) + out.shape[1:], out.dtype)
        out[groups - PAD : groups] = jnp.zeros((PAD,) + out.shape[1:], out.dtype)
    for copy in copies:
        copy.wait()
    for side, out in enumerate((first, last)):
        out[PAD + count + levels : PAD + count + 2 * levels] = edge[side].astype(jnp.float32)


def ecology(
    tracers,
    mask,
    sunlight,
    growth_max,
    half_sat,
    light_half,
    graze_max,
    graze_half,
    palatable,
    stoichiometry,
    tendency,
):
    count, levels, length, _ = tracers.shape
    grazers = count - NNUT - NPHY
    chunk = 16 if length % 16 == 0 else 8

    def level_step(level, carry):
        depth = jnp.exp(
            jnp.full((8, 128), -attenuation, jnp.float32) * (level.astype(jnp.float32) + 0.5)
        )[0:1, 0:1]
        for start in range(0, length, chunk):
            rows = pl.ds(start, chunk)
            wet = mask[level, rows].astype(jnp.float32)
            darkness = 1.0 / (sunlight[rows] * depth)
            scarcity = [1.0 / tracers[j, level, rows] for j in range(NNUT)]
            available = [None] * grazers
            eaten = None
            total_growth = None
            for k in range(NPHY):
                plant = tracers[NNUT + k, level, rows]
                worst = half_sat[0, k] * scarcity[0]
                for j in range(1, NNUT):
                    worst = jnp.maximum(worst, half_sat[j, k] * scarcity[j])
                growth = (growth_max[k] * plant) / (
                    (1.0 + worst) * (1.0 + light_half[k] * darkness)
                )
                tendency[NNUT + k, level, rows] = growth - plankton_mortality * plant
                total_growth = growth if total_growth is None else total_growth + growth
                eaten = plant if eaten is None else eaten + plant
                for z in range(grazers):
                    term = palatable[z, k] * plant
                    available[z] = term if available[z] is None else available[z] + term
            recycled = plankton_mortality * eaten - total_growth
            rates = []
            for z in range(grazers):
                grazer = tracers[NNUT + NPHY + z, level, rows]
                rate = graze_max[z] * grazer / (graze_half[z] + available[z])
                ingested = rate * available[z]
                loss = grazer_mortality * grazer * grazer
                tendency[NNUT + NPHY + z, level, rows] = wet * (assimilation * ingested - loss)
                recycled = recycled + (loss + (1.0 - assimilation) * ingested)
                rates.append(rate)
            for j in range(NNUT):
                tendency[j, level, rows] = wet * (stoichiometry[j] * recycled)
            for k in range(NPHY):
                pressure = palatable[0, k] * rates[0]
                for z in range(1, grazers):
                    pressure = pressure + palatable[z, k] * rates[z]
                plant = tracers[NNUT + k, level, rows]
                tendency[NNUT + k, level, rows] = wet * (
                    tendency[NNUT + k, level, rows] - plant * pressure
                )
        return carry

    lax.fori_loop(0, levels, level_step, 0)


def face_terms(u):
    up, down = jnp.maximum(u, 0.0), jnp.minimum(u, 0.0)
    return (
        up * (-1.0 / 6.0),
        up * (5.0 / 6.0) + down * (1.0 / 3.0),
        up * (1.0 / 3.0) + down * (5.0 / 6.0),
        down * (-1.0 / 6.0),
    )


def stencil(lower, upper):
    a0, b0, d0, e0 = face_terms(lower)
    a1, b1, d1, e1 = face_terms(upper)
    return a0, b0 - a1, 1.0 + (upper - lower) + d0 - b1, e0 - d1, -e1


def along(tracers, velocity, mask, before, after, swept, pack_left, pack_right, weights):
    count, levels, length, lanes = tracers.shape
    blocks = length // 8
    rows = lax.broadcasted_iota(jnp.int32, (length, lanes), 0)
    row8 = lax.broadcasted_iota(jnp.int32, (8, lanes), 0)
    slot = lax.broadcasted_iota(jnp.int32, (8, lanes), 1) // 2
    base = 2 * PAD

    def level_step(level, carry):
        wet = mask[level].astype(jnp.float32)
        flow = velocity[0, level]
        pick = lambda ref, field, row: ref[pl.ds(base + 2 * ((count + field) * levels + level) + row, 1)]
        wet_before, wet_after = pick(before, 1, 1), pick(after, 1, 0)
        flow_after = pick(after, 0, 0)
        wet_up = jnp.where(rows == 0, wet_before, pltpu.roll(wet, 1, 0))
        lower = flow * (wet_up * wet)
        upper = jnp.where(
            rows == length - 1,
            flow_after * (wet * wet_after),
            pltpu.roll(lower, length - 1, 0),
        )
        for n, w in enumerate(stencil(lower, upper)):
            weights[n] = w
        for block in range(blocks):
            here = pl.ds(8 * block, 8)
            wm2, wm1, w0, wp1, wp2 = [weights[n, here] for n in range(5)]
            top, bottom = block == 0, block == blocks - 1
            if top:
                zm2, zm1 = jnp.where(row8 < 2, wm2, 0.0), jnp.where(row8 < 1, wm1, 0.0)
                wm2, wm1 = jnp.where(row8 < 2, 0.0, wm2), jnp.where(row8 < 1, 0.0, wm1)
            if bottom:
                zp2, zp1 = jnp.where(row8 > 5, wp2, 0.0), jnp.where(row8 > 6, wp1, 0.0)
                wp2, wp1 = jnp.where(row8 > 5, 0.0, wp2), jnp.where(row8 > 6, 0.0, wp1)
            right = jnp.zeros((8, lanes), jnp.float32)
            left = right
            for t in range(count):
                centre = tracers[t, level, here]

                def shifted(offset):
                    if (top and offset < 0) or (bottom and offset > 0):
                        return pltpu.roll(centre, -offset % 8, 0)
                    return tracers[t, level, pl.ds(8 * block + offset, 8)]

                value = (
                    w0 * centre
                    + (wm1 * shifted(-1) + wm2 * shifted(-2))
                    + (wp1 * shifted(1) + wp2 * shifted(2))
                )
                group = base + 2 * (t * levels + level)
                if top:
                    value = value + (
                        zm2 * before[pl.ds(group, 8)] + zm1 * before[pl.ds(group + 1, 8)]
                    )
                if bottom:
                    value = value + (
                        zp2 * after[pl.ds(group - 6, 8)] + zp1 * after[pl.ds(group - 7, 8)]
                    )
                swept[t, level, here] = value
                turned = pltpu.roll(value, 2 * t + 2, 1)
                right = jnp.where(slot == t, turned, right)
                left = jnp.where(slot == t + 1, turned, left)
            across_flow = velocity[1, level, here]
            wet_here = mask[level, here].astype(jnp.float32)
            for t, value in ((count, across_flow), (count + 1, wet_here)):
                turned = pltpu.roll(value, 2 * t + 2, 1)
                right = jnp.where(slot == t, turned, right)
                left = jnp.where(slot == t + 1, turned, left)
            pack_right[level, here] = right
            pack_left[level, here] = left
        return carry

    lax.fori_loop(0, levels, level_step, 0)


def across(swept, velocity, mask, tendency, partial):
    count, levels, length, lanes = swept.shape
    blocks = length // 8
    lane = lax.broadcasted_iota(jnp.int32, (8, lanes), 1)

    def level_step(level, carry):
        for block in range(blocks):
            here = pl.ds(8 * block, 8)
            wet = mask[level, here].astype(jnp.float32)
            lower = jnp.where(lane == 0, 0.0, velocity[1, level, here] * wet * pltpu.roll(wet, 1, 1))
            upper = pltpu.roll(lower, lanes - 1, 1)
            wm2, wm1, w0, wp1, wp2 = stencil(lower, upper)
            wm2 = jnp.where(lane < 2, 0.0, wm2)
            wm1 = jnp.where(lane < 1, 0.0, wm1)
            wp1 = jnp.where(lane > lanes - 2, 0.0, wp1)
            wp2 = jnp.where(lane > lanes - 3, 0.0, wp2)
            for t in range(count):
                centre = swept[t, level, here]
                partial[t, level, here] = (
                    (tendency[t, level, here] + w0 * centre)
                    + (wm1 * pltpu.roll(centre, 1, 1) + wm2 * pltpu.roll(centre, 2, 1))
                    + (wp1 * pltpu.roll(centre, lanes - 1, 1) + wp2 * pltpu.roll(centre, lanes - 2, 1))
                )
        return carry

    lax.fori_loop(0, levels, level_step, 0)


def finish(
    partial, velocity, mask, my_left, my_right, from_left, from_right, edges, updated, even, odd, done, sems
):
    count, levels, length, lanes = partial.shape
    blocks = length // 8
    lane = lax.broadcasted_iota(jnp.int32, (8, lanes), 1)
    is_odd = lane % 2 == 1
    slot_odd = (lane // 2) % 2 == 1
    has_left, has_right = edges[0], edges[1]

    def level_step(level, carry):
        for block in range(blocks):
            here = pl.ds(8 * block, 8)
            wet = mask[level, here].astype(jnp.float32)
            flow = velocity[1, level, here]
            own_left = pltpu.roll(my_left[level, here], lanes - 2, 1)
            own_right = my_right[level, here]
            left = from_left[level, here] * has_left
            right = pltpu.roll(from_right[level, here], lanes - 2, 1) * has_right
            col = lambda value, n: jnp.broadcast_to(value[:, n : n + 1], value.shape)
            s_wet, s_flow = 2 * (count + 1), 2 * count
            wet_first, wet_last = col(wet, 0), col(wet, lanes - 1)
            u0 = col(flow, 0) * (wet_first * col(left, s_wet + 1))
            u1 = col(flow, 1) * (wet_first * col(wet, 1))
            u127 = col(flow, lanes - 1) * (wet_last * col(wet, lanes - 2))
            u128 = col(right, s_flow) * (wet_last * col(right, s_wet))
            a0, b0, d0, e0 = face_terms(u0)
            a1 = face_terms(u1)[0]
            e127 = face_terms(u127)[3]
            a128, b128, d128, e128 = face_terms(u128)
            low = (
                jnp.where(is_odd, a1, a0) * left
                + jnp.where(is_odd, 0.0, b0 - a1) * pltpu.roll(left, lanes - 1, 1)
                + jnp.where(is_odd, 0.0, d0 - u0) * own_left
                + jnp.where(is_odd, 0.0, e0) * pltpu.roll(own_left, lanes - 1, 1)
            )
            high = (
                jnp.where(is_odd, -e128, -e127) * right
                + jnp.where(is_odd, e127 - d128, 0.0) * pltpu.roll(right, 1, 1)
                + jnp.where(is_odd, u128 - b128, 0.0) * own_right
                + jnp.where(is_odd, -a128, 0.0) * pltpu.roll(own_right, 1, 1)
            )
            high = pltpu.roll(high, lanes - 2, 1)
            even[level, here] = jnp.where(slot_odd, high, low)
            odd[level, here] = jnp.where(slot_odd, low, high)
        return carry

    lax.fori_loop(0, levels, level_step, 0)
    outer = (lane < 2) | (lane > lanes - 3)
    step = max(n for n in (10, 8, 5, 4, 2, 1) if count % n == 0)
    copies = []
    for first in range(0, count, step):

        def level_add(level, carry):
            for block in range(blocks):
                here = pl.ds(8 * block, 8)
                packs = (even[level, here], odd[level, here])
                for t in range(first, first + step):
                    edge = pltpu.roll(packs[t % 2], -2 * t % lanes, 1)
                    done[t, level, here] = partial[t, level, here] + jnp.where(outer, edge, 0.0)
            return carry

        lax.fori_loop(0, levels, level_add, 0)
        part = pl.ds(first, step)
        copies.append(pltpu.make_async_copy(done.at[part], updated.at[part], sems.at[first // step]))
        copies[-1].start()
    for copy in copies:
        copy.wait()


def shards(
    tracers,
    velocity,
    land_mask,
    sunlight,
    growth_max,
    half_sat,
    light_half,
    graze_max,
    graze_half,
    palatable,
    stoichiometry,
):
    f32 = jnp.float32
    count, levels, length, lanes = tracers.shape
    tx, ty = lax.axis_size("tx"), lax.axis_size("ty")
    up = lambda n: [(i, (i + 1) % n) for i in range(n)]
    down = lambda n: [((i + 1) % n, i) for i in range(n)]
    cells = count * levels * length * lanes

    groups = 2 * PAD + (count + 2) * levels
    row_message = pltpu.VMEM((groups, 2, 1, lanes), f32)
    first, last = call(
        pack_rows,
        (row_message, row_message),
        [ANY, ANY, ANY],
        scratch=[pltpu.VMEM((2, levels, 2, 1, lanes), jnp.int32), pltpu.SemaphoreType.DMA((2, 3))],
        bytes_accessed=8 * groups * lanes,
        limit=2 << 20,
    )(
        tracers.reshape(count * levels, length, 1, lanes),
        velocity.reshape(2, levels, length, 1, lanes),
        land_mask.reshape(levels, length, 1, lanes),
    )
    first, last = first.reshape(2 * groups, lanes), last.reshape(2 * groups, lanes)
    before = lax.ppermute(last, "tx", up(tx))
    after = lax.ppermute(first, "tx", down(tx))

    held, flow, mask = in_vmem(tracers), in_vmem(velocity), in_vmem(land_mask)
    tendency = call(
        ecology,
        pltpu.VMEM(tracers.shape, f32),
        [VMEM, VMEM, VMEM] + [SMEM] * 7,
        flops=40 * cells,
        bytes_accessed=8 * cells,
        limit=2 << 20,
    )(
        held,
        mask,
        in_vmem(sunlight),
        growth_max,
        half_sat,
        light_half,
        graze_max,
        graze_half,
        palatable.astype(f32),
        stoichiometry,
    )
    column_message = pltpu.VMEM((levels, length, lanes), f32)
    swept, pack_left, pack_right = call(
        along,
        (pltpu.VMEM(tracers.shape, f32), column_message, column_message),
        [VMEM] * 5,
        scratch=[pltpu.VMEM((5, length, lanes), f32)],
        flops=20 * cells,
        bytes_accessed=8 * cells,
        limit=2 << 20,
    )(held, flow, mask, in_vmem(before), in_vmem(after))
    from_left = lax.ppermute(pack_right, "ty", up(ty))
    from_right = lax.ppermute(pack_left, "ty", down(ty))
    partial = call(
        across,
        pltpu.VMEM(tracers.shape, f32),
        [VMEM] * 4,
        flops=20 * cells,
        bytes_accessed=12 * cells,
        limit=2 << 20,
    )(swept, flow, mask, tendency)
    place = lax.axis_index("ty")
    edges = jnp.stack([place > 0, place < ty - 1]).astype(f32)
    return call(
        finish,
        jax.ShapeDtypeStruct(tracers.shape, f32),
        [VMEM] * 7 + [SMEM],
        out_specs=ANY,
        scratch=[
            pltpu.VMEM((levels, length, lanes), f32),
            pltpu.VMEM((levels, length, lanes), f32),
            pltpu.VMEM(tracers.shape, f32),
            pltpu.SemaphoreType.DMA((count,)),
        ],
        flops=4 * cells,
        bytes_accessed=8 * cells,
        limit=4 << 20,
    )(partial, flow, mask, pack_left, pack_right, in_vmem(from_left), in_vmem(from_right), edges)


def solution(mesh):
    return jax.shard_map(
        shards,
        mesh=mesh,
        in_specs=(
            P("member", None, "tx", "ty"),
            P(None, None, "tx", "ty"),
            P(None, "tx", "ty"),
            P("tx", "ty"),
            P("member"),
            P("member", None),
            P("member"),
            P("member"),
            P("member"),
            P("member", None),
            P(),
        ),
        out_specs=P("member", None, "tx", "ty"),
        check_vma=False,
    )
```

```python
import jax
import jax.numpy as jnp
from jax import lax
from jax.experimental import pallas as pl
from jax.experimental.pallas import tpu as pltpu
from jax.sharding import PartitionSpec as P


NNUT = 4
NPHY = 26
DEPTH = 12
PAD = 4

plankton_mortality = 0.05
grazer_mortality = 0.3
assimilation = 0.3
attenuation = 0.4

VMEM = pl.BlockSpec(memory_space=pltpu.VMEM)
SMEM = pl.BlockSpec(memory_space=pltpu.SMEM)
ANY = pl.BlockSpec(memory_space=pl.ANY)
HBM = pl.BlockSpec(memory_space=pltpu.HBM)


def in_vmem(array):
    return pltpu.with_memory_space_constraint(array, pltpu.VMEM)


def in_hbm(array):
    return pltpu.with_memory_space_constraint(array, pltpu.HBM)


def call(kernel, outs, specs, scratch=(), flops=0, bytes_accessed=0, limit=8 << 20, **more):
    return pl.pallas_call(
        kernel,
        out_shape=outs,
        in_specs=specs,
        scratch_shapes=list(scratch),
        cost_estimate=pl.CostEstimate(flops=flops, bytes_accessed=bytes_accessed, transcendentals=0),
        compiler_params=pltpu.CompilerParams(vmem_limit_bytes=limit),
        **more,
    )


class Deferred:
    def __init__(self, depth):
        self.depth, self.queue = depth, []

    def put(self, ref, index, value):
        self.queue.append((ref, index, value))
        if len(self.queue) > self.depth:
            self.pop()

    def pop(self):
        ref, index, value = self.queue.pop(0)
        ref[index] = value

    def flush(self):
        while self.queue:
            self.pop()


def pack_rows(tracers, velocity, mask, first, last, edge, sems):
    count, length = tracers.shape[0], tracers.shape[1]
    levels = mask.shape[0]
    copies = []
    for side, (out, start) in enumerate(((first, 0), (last, length - 2))):
        rows = pl.ds(start, 2)
        copies += [
            pltpu.make_async_copy(tracers.at[:, rows], out.at[pl.ds(PAD, count)], sems.at[side, 0]),
            pltpu.make_async_copy(
                velocity.at[0, :, rows], out.at[pl.ds(PAD + count, levels)], sems.at[side, 1]
            ),
            pltpu.make_async_copy(mask.at[:, rows], edge.at[side], sems.at[side, 2]),
        ]
    for copy in copies:
        copy.start()
    for out in (first, last):
        out[0:PAD] = jnp.zeros((PAD,) + out.shape[1:], out.dtype)
        out[PAD + count + 2 * levels :] = jnp.zeros_like(out[PAD + count + 2 * levels :])
    for copy in copies:
        copy.wait()
    for side, out in enumerate((first, last)):
        out[PAD + count + levels : PAD + count + 2 * levels] = edge[side].astype(jnp.float32)


def ecology(
    tracers,
    mask,
    sunlight,
    growth_max,
    half_sat,
    light_half,
    graze_max,
    graze_half,
    palatable,
    stoichiometry,
    tendency,
):
    count, levels, length, _ = tracers.shape
    grazers = count - NNUT - NPHY
    chunk = 16 if length % 16 == 0 else 8

    def level_step(level, carry):
        depth = jnp.exp(
            jnp.full((8, 128), -attenuation, jnp.float32) * (level.astype(jnp.float32) + 0.5)
        )[0:1, 0:1]
        for start in range(0, length, chunk):
            rows = pl.ds(start, chunk)
            wet = mask[level, rows].astype(jnp.float32)
            darkness = 1.0 / (sunlight[rows] * depth)
            scarcity = [1.0 / tracers[j, level, rows] for j in range(NNUT)]
            available = [None] * grazers
            eaten = None
            total_growth = None
            for k in range(NPHY):
                plant = tracers[NNUT + k, level, rows]
                worst = half_sat[0, k] * scarcity[0]
                for j in range(1, NNUT):
                    worst = jnp.maximum(worst, half_sat[j, k] * scarcity[j])
                growth = (growth_max[k] * plant) / (
                    (1.0 + worst) * (1.0 + light_half[k] * darkness)
                )
                tendency[NNUT + k, level, rows] = growth - plankton_mortality * plant
                total_growth = growth if total_growth is None else total_growth + growth
                eaten = plant if eaten is None else eaten + plant
                for z in range(grazers):
                    term = palatable[z, k] * plant
                    available[z] = term if available[z] is None else available[z] + term
            recycled = plankton_mortality * eaten - total_growth
            rates = []
            for z in range(grazers):
                grazer = tracers[NNUT + NPHY + z, level, rows]
                rate = graze_max[z] * grazer / (graze_half[z] + available[z])
                ingested = rate * available[z]
                loss = grazer_mortality * grazer * grazer
                tendency[NNUT + NPHY + z, level, rows] = wet * (assimilation * ingested - loss)
                recycled = recycled + (loss + (1.0 - assimilation) * ingested)
                rates.append(rate)
            for j in range(NNUT):
                tendency[j, level, rows] = wet * (stoichiometry[j] * recycled)
            for k in range(NPHY):
                pressure = palatable[0, k] * rates[0]
                for z in range(1, grazers):
                    pressure = pressure + palatable[z, k] * rates[z]
                plant = tracers[NNUT + k, level, rows]
                tendency[NNUT + k, level, rows] = wet * (
                    tendency[NNUT + k, level, rows] - plant * pressure
                )
        return carry

    lax.fori_loop(0, levels, level_step, 0)


def face_terms(u):
    up, down = jnp.maximum(u, 0.0), jnp.minimum(u, 0.0)
    return (
        up * (-1.0 / 6.0),
        up * (5.0 / 6.0) + down * (1.0 / 3.0),
        up * (1.0 / 3.0) + down * (5.0 / 6.0),
        down * (-1.0 / 6.0),
    )


def stencil(lower, upper):
    a0, b0, d0, e0 = face_terms(lower)
    a1, b1, d1, e1 = face_terms(upper)
    return a0, b0 - a1, 1.0 + (upper - lower) + d0 - b1, e0 - d1, -e1


def row_weights(velocity, mask, level, wet_before, wet_after, flow_after):
    length, lanes = mask.shape[1:]
    rows = lax.broadcasted_iota(jnp.int32, (length, lanes), 0)
    wet = mask[level].astype(jnp.float32)
    wet_up = jnp.where(rows == 0, wet_before, pltpu.roll(wet, 1, 0))
    lower = velocity[0, level] * (wet_up * wet)
    upper = jnp.where(
        rows == length - 1, flow_after * (wet * wet_after), pltpu.roll(lower, length - 1, 0)
    )
    return stencil(lower, upper)


def column_weights(velocity, mask, level, here):
    lanes = mask.shape[2]
    lane = lax.broadcasted_iota(jnp.int32, (8, lanes), 1)
    wet = mask[level, here].astype(jnp.float32)
    lower = jnp.where(lane == 0, 0.0, velocity[1, level, here] * wet * pltpu.roll(wet, 1, 1))
    upper = pltpu.roll(lower, lanes - 1, 1)
    wm2, wm1, w0, wp1, wp2 = stencil(lower, upper)
    return (
        jnp.where(lane < 2, 0.0, wm2),
        jnp.where(lane < 1, 0.0, wm1),
        w0,
        jnp.where(lane > lanes - 2, 0.0, wp1),
        jnp.where(lane > lanes - 3, 0.0, wp2),
    )


def sweep_across(centre, weights):
    wm2, wm1, w0, wp1, wp2 = weights
    lanes = centre.shape[1]
    return (
        w0 * centre
        + (wm1 * pltpu.roll(centre, 1, 1) + wm2 * pltpu.roll(centre, 2, 1))
        + (wp1 * pltpu.roll(centre, lanes - 1, 1) + wp2 * pltpu.roll(centre, lanes - 2, 1))
    )


class Packer:
    def __init__(self, lanes):
        self.slot = lax.broadcasted_iota(jnp.int32, (8, lanes), 1) // 2
        self.left = self.right = jnp.zeros((8, lanes), jnp.float32)

    def add(self, t, value):
        turned = pltpu.roll(value, 2 * t + 2, 1)
        self.right = jnp.where(self.slot == t, turned, self.right)
        self.left = jnp.where(self.slot == t + 1, turned, self.left)


def pack_forcing(packer, count, velocity, mask, level, here):
    packer.add(count, velocity[1, level, here])
    packer.add(count + 1, mask[level, here].astype(jnp.float32))


def interior(tracers, velocity, mask, _, partial, pack_left, pack_right, weights):
    count, levels, length, lanes = tracers.shape
    zero = jnp.zeros((1, lanes), jnp.float32)

    def level_step(level, carry):
        for n, w in enumerate(row_weights(velocity, mask, level, zero, zero, zero)):
            weights[n] = w

        def block_step(block, carry):
            begin = pl.multiple_of(8 * block, 8)
            here = pl.ds(begin, 8)
            wm2, wm1, w0, wp1, wp2 = [weights[n, here] for n in range(5)]
            columns = column_weights(velocity, mask, level, here)
            packer = Packer(lanes)
            later = Deferred(DEPTH)
            for t in range(count):
                at = lambda offset: tracers[t, level, pl.ds(begin + offset, 8)]
                value = (
                    w0 * at(0) + (wm1 * at(-1) + wm2 * at(-2)) + (wp1 * at(1) + wp2 * at(2))
                )
                packer.add(t, value)
                later.put(
                    partial, (t, level, here), partial[t, level, here] + sweep_across(value, columns)
                )
            pack_forcing(packer, count, velocity, mask, level, here)
            later.flush()
            pack_right[level, here] = packer.right
            pack_left[level, here] = packer.left
            return carry

        return lax.fori_loop(1, length // 8 - 1, block_step, carry)

    lax.fori_loop(0, levels, level_step, 0)


def border(
    tracers, velocity, mask, before, after, partial, left_in, right_in, swept, pack_left, pack_right, through
):
    count, levels, length, lanes = tracers.shape
    row8 = lax.broadcasted_iota(jnp.int32, (8, lanes), 0)
    base = 2 * PAD

    def level_step(level, carry):
        pick = lambda ref, field, row: ref[pl.ds(base + 2 * ((count + field) * levels + level) + row, 1)]
        weights = row_weights(
            velocity, mask, level, pick(before, 1, 1), pick(after, 1, 0), pick(after, 0, 0)
        )
        for side, first in enumerate((0, length - 8)):
            here = pl.ds(first, 8)
            wm2, wm1, w0, wp1, wp2 = [w[first : first + 8] for w in weights]
            if side == 0:
                z2, z1 = jnp.where(row8 < 2, wm2, 0.0), jnp.where(row8 < 1, wm1, 0.0)
                wm2, wm1 = jnp.where(row8 < 2, 0.0, wm2), jnp.where(row8 < 1, 0.0, wm1)
            else:
                z2, z1 = jnp.where(row8 > 5, wp2, 0.0), jnp.where(row8 > 6, wp1, 0.0)
                wp2, wp1 = jnp.where(row8 > 5, 0.0, wp2), jnp.where(row8 > 6, 0.0, wp1)
            packer = Packer(lanes)
            later = Deferred(DEPTH)
            for t in range(count):
                centre = tracers[t, level, here]

                def at(offset):
                    if (offset < 0) == (side == 0):
                        return pltpu.roll(centre, -offset % 8, 0)
                    return tracers[t, level, pl.ds(first + offset, 8)]

                group = base + 2 * (t * levels + level)
                if side == 0:
                    beyond = z2 * before[pl.ds(group, 8)] + z1 * before[pl.ds(group + 1, 8)]
                else:
                    beyond = z2 * after[pl.ds(group - 6, 8)] + z1 * after[pl.ds(group - 7, 8)]
                value = (
                    (w0 * centre + beyond) + (wm1 * at(-1) + wm2 * at(-2)) + (wp1 * at(1) + wp2 * at(2))
                )
                later.put(swept, (t, level, pl.ds(8 * side, 8)), value)
                packer.add(t, value)
            pack_forcing(packer, count, velocity, mask, level, here)
            later.flush()
            pack_right[level, here] = packer.right
            pack_left[level, here] = packer.left
        return carry

    lax.fori_loop(0, levels, level_step, 0)


def border_across(swept, velocity, mask, _, partial):
    count, levels = swept.shape[:2]
    length = mask.shape[1]

    def step(index, carry):
        level, side = index // 2, index % 2
        here = pl.ds(pl.multiple_of(side * (length - 8), 8), 8)
        columns = column_weights(velocity, mask, level, here)
        later = Deferred(DEPTH)
        for t in range(count):
            value = swept[t, level, pl.ds(pl.multiple_of(8 * side, 8), 8)]
            later.put(partial, (t, level, here), partial[t, level, here] + sweep_across(value, columns))
        later.flush()
        return carry

    lax.fori_loop(0, 2 * levels, step, 0)


def finish(
    partial, velocity, mask, my_left, my_right, from_left, from_right, edges, done, updated, even, odd, sems
):
    count, levels, length, lanes = done.shape
    blocks = length // 8
    lane = lax.broadcasted_iota(jnp.int32, (8, lanes), 1)
    is_odd = lane % 2 == 1
    slot_odd = (lane // 2) % 2 == 1
    has_left, has_right = edges[0], edges[1]

    def level_step(level, carry):
        for block in range(blocks):
            here = pl.ds(8 * block, 8)
            wet = mask[level, here].astype(jnp.float32)
            flow = velocity[1, level, here]
            own_left = pltpu.roll(my_left[level, here], lanes - 2, 1)
            own_right = my_right[level, here]
            left = from_left[level, here] * has_left
            right = pltpu.roll(from_right[level, here], lanes - 2, 1) * has_right
            col = lambda value, n: jnp.broadcast_to(value[:, n : n + 1], value.shape)
            s_wet, s_flow = 2 * (count + 1), 2 * count
            wet_first, wet_last = col(wet, 0), col(wet, lanes - 1)
            u0 = col(flow, 0) * (wet_first * col(left, s_wet + 1))
            u1 = col(flow, 1) * (wet_first * col(wet, 1))
            u127 = col(flow, lanes - 1) * (wet_last * col(wet, lanes - 2))
            u128 = col(right, s_flow) * (wet_last * col(right, s_wet))
            a0, b0, d0, e0 = face_terms(u0)
            a1 = face_terms(u1)[0]
            e127 = face_terms(u127)[3]
            a128, b128, d128, e128 = face_terms(u128)
            low = (
                jnp.where(is_odd, a1, a0) * left
                + jnp.where(is_odd, 0.0, b0 - a1) * pltpu.roll(left, lanes - 1, 1)
                + jnp.where(is_odd, 0.0, d0 - u0) * own_left
                + jnp.where(is_odd, 0.0, e0) * pltpu.roll(own_left, lanes - 1, 1)
            )
            high = (
                jnp.where(is_odd, -e128, -e127) * right
                + jnp.where(is_odd, e127 - d128, 0.0) * pltpu.roll(right, 1, 1)
                + jnp.where(is_odd, u128 - b128, 0.0) * own_right
                + jnp.where(is_odd, -a128, 0.0) * pltpu.roll(own_right, 1, 1)
            )
            high = pltpu.roll(high, lanes - 2, 1)
            even[level, here] = jnp.where(slot_odd, high, low)
            odd[level, here] = jnp.where(slot_odd, low, high)
        return carry

    lax.fori_loop(0, levels, level_step, 0)
    outer = (lane < 2) | (lane > lanes - 3)
    step = max(n for n in (4, 2, 1) if count % n == 0)

    def copy(chunk):
        part = pl.ds(chunk * step, step)
        return pltpu.make_async_copy(done.at[part], updated.at[part], sems.at[chunk])

    for chunk in range(count // step):
        for level in range(levels):
            for block in range(blocks):
                here = pl.ds(8 * block, 8)
                packs = (even[level, here], odd[level, here])
                for t in range(chunk * step, chunk * step + step):
                    edge = pltpu.roll(packs[t % 2], (lanes - 2 * t) % lanes, 1)
                    done[t, level, here] = done[t, level, here] + jnp.where(outer, edge, 0.0)
        copy(chunk).start()
    for chunk in range(count // step):
        copy(chunk).wait()


def shards(
    tracers,
    velocity,
    land_mask,
    sunlight,
    growth_max,
    half_sat,
    light_half,
    graze_max,
    graze_half,
    palatable,
    stoichiometry,
):
    f32 = jnp.float32
    count, levels, length, lanes = tracers.shape
    tx, ty = lax.axis_size("tx"), lax.axis_size("ty")
    up = lambda n: [(i, (i + 1) % n) for i in range(n)]
    down = lambda n: [((i + 1) % n, i) for i in range(n)]
    cells = count * levels * length * lanes

    assert length % 8 == 0 and length >= 16 and 2 * count + 6 <= lanes
    groups = -(-(2 * PAD + (count + 2) * levels) // 4) * 4
    row_message = pltpu.VMEM((groups, 2, 1, lanes), f32)
    first, last = call(
        pack_rows,
        (row_message, row_message),
        [HBM, HBM, HBM],
        scratch=[pltpu.VMEM((2, levels, 2, 1, lanes), jnp.int32), pltpu.SemaphoreType.DMA((2, 3))],
        bytes_accessed=8 * groups * lanes,
        limit=2 << 20,
    )(
        in_hbm(tracers.reshape(count * levels, length, 1, lanes)),
        in_hbm(velocity.reshape(2, levels, length, 1, lanes)),
        in_hbm(land_mask.reshape(levels, length, 1, lanes)),
    )
    first, last = first.reshape(2 * groups, lanes), last.reshape(2 * groups, lanes)
    before = lax.ppermute(last, "tx", up(tx))
    after = lax.ppermute(first, "tx", down(tx))

    held, flow, mask = in_vmem(tracers), in_vmem(velocity), in_vmem(land_mask)
    field = pltpu.VMEM(tracers.shape, f32)
    columns = pltpu.VMEM((levels, length, lanes), f32)
    tendency = call(
        ecology,
        field,
        [VMEM, VMEM, VMEM] + [SMEM] * 7,
        flops=40 * cells,
        bytes_accessed=8 * cells,
        limit=2 << 20,
    )(
        held,
        mask,
        in_vmem(sunlight),
        growth_max,
        half_sat,
        light_half,
        graze_max,
        graze_half,
        palatable.astype(f32),
        stoichiometry,
    )
    partial, pack_left, pack_right = call(
        interior,
        (field, columns, columns),
        [VMEM] * 4,
        scratch=[pltpu.VMEM((5, length, lanes), f32)],
        flops=20 * cells,
        bytes_accessed=8 * cells,
        limit=2 << 20,
        input_output_aliases={3: 0},
    )(held, flow, mask, tendency)
    swept, pack_left, pack_right, partial = call(
        border,
        (pltpu.VMEM((count, levels, 16, lanes), f32), columns, columns, field),
        [VMEM] * 5 + [ANY] * 3,
        out_specs=[VMEM] * 3 + [ANY],
        flops=10 * cells,
        bytes_accessed=8 * cells,
        limit=2 << 20,
        input_output_aliases={5: 3, 6: 1, 7: 2},
    )(held, flow, mask, in_vmem(before), in_vmem(after), partial, pack_left, pack_right)
    from_left = lax.ppermute(pack_right, "ty", up(ty))
    from_right = lax.ppermute(pack_left, "ty", down(ty))
    partial = call(
        border_across,
        field,
        [VMEM] * 4,
        flops=10 * cells,
        bytes_accessed=6 * cells,
        limit=2 << 20,
        input_output_aliases={3: 0},
    )(swept, flow, mask, partial)
    place = lax.axis_index("ty")
    edges = jnp.stack([place > 0, place < ty - 1]).astype(f32)
    return call(
        finish,
        (field, jax.ShapeDtypeStruct(tracers.shape, f32)),
        [VMEM] * 7 + [SMEM],
        out_specs=[VMEM, HBM],
        input_output_aliases={0: 0},
        scratch=[
            pltpu.VMEM((levels, length, lanes), f32),
            pltpu.VMEM((levels, length, lanes), f32),
            pltpu.SemaphoreType.DMA((count,)),
        ],
        flops=4 * cells,
        bytes_accessed=8 * cells,
        limit=4 << 20,
    )(partial, flow, mask, pack_left, pack_right, in_vmem(from_left), in_vmem(from_right), edges)[1]


def solution(mesh):
    return jax.shard_map(
        shards,
        mesh=mesh,
        in_specs=(
            P("member", None, "tx", "ty"),
            P(None, None, "tx", "ty"),
            P(None, "tx", "ty"),
            P("tx", "ty"),
            P("member"),
            P("member", None),
            P("member"),
            P("member"),
            P("member"),
            P("member", None),
            P(),
        ),
        out_specs=P("member", None, "tx", "ty"),
        check_vma=False,
    )
```

```python
import jax
import jax.numpy as jnp
from jax import lax
from jax.experimental import pallas as pl
from jax.experimental.pallas import tpu as pltpu
from jax.sharding import PartitionSpec as P


NNUT = 4
NPHY = 26
DEPTH = 12
PAD = 4

plankton_mortality = 0.05
grazer_mortality = 0.3
assimilation = 0.3
attenuation = 0.4

VMEM = pl.BlockSpec(memory_space=pltpu.VMEM)
SMEM = pl.BlockSpec(memory_space=pltpu.SMEM)
ANY = pl.BlockSpec(memory_space=pl.ANY)
HBM = pl.BlockSpec(memory_space=pltpu.HBM)


def in_vmem(array):
    return pltpu.with_memory_space_constraint(array, pltpu.VMEM)


def in_hbm(array):
    return pltpu.with_memory_space_constraint(array, pltpu.HBM)


def call(kernel, outs, specs, scratch=(), flops=0, bytes_accessed=0, limit=8 << 20, **more):
    return pl.pallas_call(
        kernel,
        out_shape=outs,
        in_specs=specs,
        scratch_shapes=list(scratch),
        cost_estimate=pl.CostEstimate(flops=flops, bytes_accessed=bytes_accessed, transcendentals=0),
        compiler_params=pltpu.CompilerParams(vmem_limit_bytes=limit),
        **more,
    )


class Deferred:
    def __init__(self, depth):
        self.depth, self.queue = depth, []

    def put(self, ref, index, value):
        self.queue.append((ref, index, value))
        if len(self.queue) > self.depth:
            self.pop()

    def pop(self):
        ref, index, value = self.queue.pop(0)
        ref[index] = value

    def flush(self):
        while self.queue:
            self.pop()


def diet_matrices(palatable, to_grazers, to_plants):
    f32, bf16 = jnp.float32, jnp.bfloat16
    grazers = palatable.shape[0]

    def picks(shape, dim, period):
        index = lax.broadcasted_iota(jnp.int32, shape, dim)
        other = lax.broadcasted_iota(jnp.int32, shape, 1 - dim)
        return ((index % period) // 8 == other).astype(f32).astype(bf16)

    def spread(left, middle, right, transposed):
        dims = (((1,), (1 if transposed else 0,)), ((), ()))
        part = lax.dot_general(left, middle, dims, preferred_element_type=f32).astype(bf16)
        whole = jnp.dot(part, right, preferred_element_type=f32)
        row = lax.broadcasted_iota(jnp.int32, whole.shape, 0) % 8
        col = lax.broadcasted_iota(jnp.int32, whole.shape, 1) % 8
        return jnp.where(row == col, whole, 0.0).astype(bf16)

    eats = palatable[...].astype(f32).astype(bf16)
    rows_z, rows_k = 8 * grazers, 8 * NPHY
    to_grazers[...] = spread(
        picks((rows_z, grazers), 0, rows_z), eats, picks((NPHY, 2 * rows_k), 1, rows_k), False
    )
    to_plants[...] = spread(
        picks((rows_k, NPHY), 0, rows_k), eats, picks((grazers, 2 * rows_z), 1, rows_z), True
    )


def pack_rows(tracers, velocity, mask, first, last, edge, sems):
    count, length = tracers.shape[0], tracers.shape[1]
    levels = mask.shape[0]
    copies = []
    for side, (out, start) in enumerate(((first, 0), (last, length - 2))):
        rows = pl.ds(start, 2)
        copies += [
            pltpu.make_async_copy(tracers.at[:, rows], out.at[pl.ds(PAD, count)], sems.at[side, 0]),
            pltpu.make_async_copy(
                velocity.at[0, :, rows], out.at[pl.ds(PAD + count, levels)], sems.at[side, 1]
            ),
            pltpu.make_async_copy(mask.at[:, rows], edge.at[side], sems.at[side, 2]),
        ]
    for copy in copies:
        copy.start()
    for out in (first, last):
        out[0:PAD] = jnp.zeros((PAD,) + out.shape[1:], out.dtype)
        out[PAD + count + 2 * levels :] = jnp.zeros_like(out[PAD + count + 2 * levels :])
    for copy in copies:
        copy.wait()
    for side, out in enumerate((first, last)):
        out[PAD + count + levels : PAD + count + 2 * levels] = edge[side].astype(jnp.float32)


def ecology(
    tracers,
    mask,
    sunlight,
    palatable,
    growth_max,
    half_sat,
    light_half,
    graze_max,
    graze_half,
    stoichiometry,
    tendency,
    to_grazers,
    to_plants,
):
    count, levels, length, lanes = tracers.shape
    grazers = count - NNUT - NPHY
    f32, bf16 = jnp.float32, jnp.bfloat16
    plants = pl.ds(NNUT, NPHY)

    diet_matrices(palatable, to_grazers, to_plants)

    def split(values):
        wide = jnp.concatenate([v.reshape(-1, lanes) for v in values], axis=1)
        high = wide.astype(bf16)
        return jnp.concatenate([high, (wide - high.astype(f32)).astype(bf16)], axis=0)

    def entry(wide, n):
        part = wide[8 * n : 8 * n + 8]
        return jnp.concatenate([part[:, :lanes], part[:, lanes:]], axis=0)

    def level_step(level, carry):
        depth = jnp.exp(jnp.full((8, 128), -attenuation, f32) * (level.astype(f32) + 0.5))[0:1, 0:1]
        for start in range(0, length, 16):
            rows = pl.ds(start, 16)
            halves = (pl.ds(start, 8), pl.ds(start + 8, 8))
            available = jnp.dot(
                to_grazers[...],
                split([tracers[plants, level, half] for half in halves]),
                preferred_element_type=f32,
            )
            wet = mask[level, rows].astype(f32)
            recycled = jnp.zeros((16, lanes), f32)
            rates = []
            later = Deferred(DEPTH)
            for z in range(grazers):
                grazer = tracers[NNUT + NPHY + z, level, rows]
                prey = entry(available, z)
                rate = graze_max[z] * grazer / (graze_half[z] + prey)
                ingested = rate * prey
                loss = grazer_mortality * grazer * grazer
                later.put(
                    tendency,
                    (NNUT + NPHY + z, level, rows),
                    wet * (assimilation * ingested - loss),
                )
                recycled = recycled + (loss + (1.0 - assimilation) * ingested)
                rates.append(rate)
            pressure = jnp.dot(
                to_plants[...],
                split([jnp.concatenate([r[n : n + 8] for r in rates], axis=0) for n in (0, 8)]),
                preferred_element_type=f32,
            )
            darkness = 1.0 / (sunlight[rows] * depth)
            scarcity = [1.0 / tracers[j, level, rows] for j in range(NNUT)]
            for k in range(NPHY):
                plant = tracers[NNUT + k, level, rows]
                worst = half_sat[0, k] * scarcity[0]
                for j in range(1, NNUT):
                    worst = jnp.maximum(worst, half_sat[j, k] * scarcity[j])
                growth = (growth_max[k] * plant) / (
                    (1.0 + worst) * (1.0 + light_half[k] * darkness)
                )
                recycled = recycled + (plankton_mortality * plant - growth)
                later.put(
                    tendency,
                    (NNUT + k, level, rows),
                    wet * (growth - plant * (entry(pressure, k) + plankton_mortality)),
                )
            for j in range(NNUT):
                later.put(tendency, (j, level, rows), wet * (stoichiometry[j] * recycled))
            later.flush()
        return carry

    lax.fori_loop(0, levels, level_step, 0)


def face_terms(u):
    up, down = jnp.maximum(u, 0.0), jnp.minimum(u, 0.0)
    return (
        up * (-1.0 / 6.0),
        up * (5.0 / 6.0) + down * (1.0 / 3.0),
        up * (1.0 / 3.0) + down * (5.0 / 6.0),
        down * (-1.0 / 6.0),
    )


def stencil(lower, upper):
    a0, b0, d0, e0 = face_terms(lower)
    a1, b1, d1, e1 = face_terms(upper)
    return a0, b0 - a1, 1.0 + (upper - lower) + d0 - b1, e0 - d1, -e1


def row_weights(velocity, mask, level, wet_before, wet_after, flow_after):
    length, lanes = mask.shape[1:]
    rows = lax.broadcasted_iota(jnp.int32, (length, lanes), 0)
    wet = mask[level].astype(jnp.float32)
    wet_up = jnp.where(rows == 0, wet_before, pltpu.roll(wet, 1, 0))
    lower = velocity[0, level] * (wet_up * wet)
    upper = jnp.where(
        rows == length - 1, flow_after * (wet * wet_after), pltpu.roll(lower, length - 1, 0)
    )
    return stencil(lower, upper)


def column_weights(velocity, mask, level, here):
    lanes = mask.shape[2]
    lane = lax.broadcasted_iota(jnp.int32, (8, lanes), 1)
    wet = mask[level, here].astype(jnp.float32)
    lower = jnp.where(lane == 0, 0.0, velocity[1, level, here] * wet * pltpu.roll(wet, 1, 1))
    upper = pltpu.roll(lower, lanes - 1, 1)
    wm2, wm1, w0, wp1, wp2 = stencil(lower, upper)
    return (
        jnp.where(lane < 2, 0.0, wm2),
        jnp.where(lane < 1, 0.0, wm1),
        w0,
        jnp.where(lane > lanes - 2, 0.0, wp1),
        jnp.where(lane > lanes - 3, 0.0, wp2),
    )


def sweep_across(centre, weights):
    wm2, wm1, w0, wp1, wp2 = weights
    lanes = centre.shape[1]
    return (
        w0 * centre
        + (wm1 * pltpu.roll(centre, 1, 1) + wm2 * pltpu.roll(centre, 2, 1))
        + (wp1 * pltpu.roll(centre, lanes - 1, 1) + wp2 * pltpu.roll(centre, lanes - 2, 1))
    )


class Packer:
    def __init__(self, count, velocity, mask, level, here):
        wet = mask[level, here].astype(jnp.float32)
        lane = lax.broadcasted_iota(jnp.int32, wet.shape, 1)
        self.slot = lane // 2
        self.left = self.right = jnp.zeros_like(wet)
        self.add(count, jnp.where(lane < 2, velocity[1, level, here] * wet, wet))

    def add(self, t, value):
        turned = pltpu.roll(value, 2 * t + 2, 1)
        self.right = jnp.where(self.slot == t, turned, self.right)
        self.left = jnp.where(self.slot == t + 1, turned, self.left)


def interior(tracers, velocity, mask, _, partial, pack_left, pack_right, weights):
    count, levels, length, lanes = tracers.shape
    zero = jnp.zeros((1, lanes), jnp.float32)

    def level_step(level, carry):
        for n, w in enumerate(row_weights(velocity, mask, level, zero, zero, zero)):
            weights[n] = w

        def block_step(block, carry):
            begin = pl.multiple_of(8 * block, 8)
            here = pl.ds(begin, 8)
            wm2, wm1, w0, wp1, wp2 = [weights[n, here] for n in range(5)]
            columns = column_weights(velocity, mask, level, here)
            packer = Packer(count, velocity, mask, level, here)
            later = Deferred(DEPTH)
            for t in range(count):
                at = lambda offset: tracers[t, level, pl.ds(begin + offset, 8)]
                value = (
                    w0 * at(0) + (wm1 * at(-1) + wm2 * at(-2)) + (wp1 * at(1) + wp2 * at(2))
                )
                packer.add(t, value)
                later.put(
                    partial, (t, level, here), partial[t, level, here] + sweep_across(value, columns)
                )
            later.flush()
            pack_right[level, here] = packer.right
            pack_left[level, here] = packer.left
            return carry

        return lax.fori_loop(1, length // 8 - 1, block_step, carry)

    lax.fori_loop(0, levels, level_step, 0)


def border(
    tracers, velocity, mask, before, after, partial, left_in, right_in, swept, pack_left, pack_right, through
):
    count, levels, length, lanes = tracers.shape
    row8 = lax.broadcasted_iota(jnp.int32, (8, lanes), 0)
    base = 2 * PAD

    def level_step(level, carry):
        pick = lambda ref, field, row: ref[pl.ds(base + 2 * ((count + field) * levels + level) + row, 1)]
        weights = row_weights(
            velocity, mask, level, pick(before, 1, 1), pick(after, 1, 0), pick(after, 0, 0)
        )
        for side, first in enumerate((0, length - 8)):
            here = pl.ds(first, 8)
            wm2, wm1, w0, wp1, wp2 = [w[first : first + 8] for w in weights]
            if side == 0:
                z2, z1 = jnp.where(row8 < 2, wm2, 0.0), jnp.where(row8 < 1, wm1, 0.0)
                wm2, wm1 = jnp.where(row8 < 2, 0.0, wm2), jnp.where(row8 < 1, 0.0, wm1)
            else:
                z2, z1 = jnp.where(row8 > 5, wp2, 0.0), jnp.where(row8 > 6, wp1, 0.0)
                wp2, wp1 = jnp.where(row8 > 5, 0.0, wp2), jnp.where(row8 > 6, 0.0, wp1)
            packer = Packer(count, velocity, mask, level, here)
            later = Deferred(DEPTH)
            for t in range(count):
                centre = tracers[t, level, here]

                def at(offset):
                    if (offset < 0) == (side == 0):
                        return pltpu.roll(centre, -offset % 8, 0)
                    return tracers[t, level, pl.ds(first + offset, 8)]

                group = base + 2 * (t * levels + level)
                if side == 0:
                    beyond = z2 * before[pl.ds(group, 8)] + z1 * before[pl.ds(group + 1, 8)]
                else:
                    beyond = z2 * after[pl.ds(group - 6, 8)] + z1 * after[pl.ds(group - 7, 8)]
                value = (
                    (w0 * centre + beyond) + (wm1 * at(-1) + wm2 * at(-2)) + (wp1 * at(1) + wp2 * at(2))
                )
                later.put(swept, (t, level, pl.ds(8 * side, 8)), value)
                packer.add(t, value)
            later.flush()
            pack_right[level, here] = packer.right
            pack_left[level, here] = packer.left
        return carry

    lax.fori_loop(0, levels, level_step, 0)


PREPARED = 8


def border_across(swept, velocity, mask, my_left, my_right, _, partial, ready):
    count, levels, _, lanes = swept.shape
    length = mask.shape[1]
    place, size = lax.axis_index("ty"), lax.axis_size("ty")
    has_left = jnp.where(place > 0, 1.0, 0.0)
    has_right = jnp.where(place < size - 1, 1.0, 0.0)
    col = lambda value, n: jnp.broadcast_to(value[:, n : n + 1], value.shape)

    def step(index, carry):
        level, side = index // 2, index % 2
        here = pl.ds(pl.multiple_of(side * (length - 8), 8), 8)
        columns = column_weights(velocity, mask, level, here)
        later = Deferred(DEPTH)
        for t in range(count):
            value = swept[t, level, pl.ds(pl.multiple_of(8 * side, 8), 8)]
            later.put(partial, (t, level, here), partial[t, level, here] + sweep_across(value, columns))
        later.flush()
        return carry

    lax.fori_loop(0, 2 * levels, step, 0)

    def prepare(level, carry):
        for block in range(length // 8):
            here = pl.ds(8 * block, 8)
            wet = mask[level, here].astype(jnp.float32)
            flow = velocity[1, level, here]
            opened = flow * wet * pltpu.roll(wet, 1, 1)
            left, right = my_left[level, here], my_right[level, here]
            arrays = (
                col(flow * wet, 0) * has_left,
                col(wet, lanes - 1) * has_right,
                face_terms(col(opened, 1))[0] * has_left,
                face_terms(col(opened, lanes - 1))[3] * has_right,
                pltpu.roll(left, lanes - 2, 1),
                pltpu.roll(left, lanes - 3, 1),
                pltpu.roll(right, lanes - 2, 1),
                pltpu.roll(right, lanes - 1, 1),
            )
            for n, array in enumerate(arrays):
                ready[n, level, here] = array
        return carry

    lax.fori_loop(0, levels, prepare, 0)


def finish(ready, from_left, from_right, _, done, updated, even, odd, sems):
    count, levels, length, lanes = done.shape
    blocks = length // 8
    lane = lax.broadcasted_iota(jnp.int32, (8, lanes), 1)
    is_odd = lane % 2 == 1
    slot_odd = (lane // 2) % 2 == 1
    col = lambda value, n: jnp.broadcast_to(value[:, n : n + 1], value.shape)

    def level_step(level, carry):
        for block in range(blocks):
            here = pl.ds(8 * block, 8)
            open_low, open_high, a1, e127, s0, s1, s127, s126 = (
                ready[n, level, here] for n in range(PREPARED)
            )
            left, right = from_left[level, here], pltpu.roll(from_right[level, here], lanes - 4, 1)
            u0 = open_low * col(left, 2 * count + 1)
            u128 = open_high * col(right, 2 * count - 2)
            a0, b0, d0, e0 = face_terms(u0)
            a128, b128, d128, e128 = face_terms(u128)
            low = jnp.where(is_odd, a1, a0) * left + jnp.where(
                is_odd,
                0.0,
                (b0 - a1) * pltpu.roll(left, lanes - 1, 1) + ((d0 - u0) * s0 + e0 * s1),
            )
            high = jnp.where(
                is_odd,
                (e127 - d128) * pltpu.roll(right, 1, 1) + ((u128 - b128) * s127 - a128 * s126),
                0.0,
            ) - jnp.where(is_odd, e128, e127) * right
            even[level, here] = jnp.where(slot_odd, high, low)
            odd[level, here] = jnp.where(slot_odd, low, high)
        return carry

    lax.fori_loop(0, levels, level_step, 0)
    outer = (lane < 2) | (lane > lanes - 3)
    step = 8 if count % 8 == 0 else 2

    def copy(chunk):
        part = pl.ds(chunk * step, step)
        return pltpu.make_async_copy(done.at[part], updated.at[part], sems.at[chunk])

    def add(chunk, carry):
        start = chunk * step
        turns = [jnp.where(start + n == 0, 0, lanes - 2 * (start + n)) for n in range(step)]
        later = Deferred(2 * DEPTH)
        for level in range(levels):
            for block in range(blocks):
                here = pl.ds(8 * block, 8)
                packs = (even[level, here], odd[level, here])
                for n in range(step):
                    edge = pltpu.roll(packs[n % 2], turns[n], 1)
                    at = (start + n, level, here)
                    later.put(done, at, done[at] + jnp.where(outer, edge, 0.0))
        later.flush()
        copy(chunk).start()
        return carry

    def wait(chunk, carry):
        copy(chunk).wait()
        return carry

    lax.fori_loop(0, count // step, add, 0)
    lax.fori_loop(0, count // step, wait, 0)


def shards(
    tracers,
    velocity,
    land_mask,
    sunlight,
    growth_max,
    half_sat,
    light_half,
    graze_max,
    graze_half,
    palatable,
    stoichiometry,
):
    f32 = jnp.float32
    count, levels, length, lanes = tracers.shape
    tx, ty = lax.axis_size("tx"), lax.axis_size("ty")
    up = lambda n: [(i, (i + 1) % n) for i in range(n)]
    down = lambda n: [((i + 1) % n, i) for i in range(n)]
    cells = count * levels * length * lanes

    assert length % 16 == 0 and count % 2 == 0 and 2 * count + 4 <= lanes
    groups = -(-(2 * PAD + (count + 2) * levels) // 4) * 4
    row_message = pltpu.VMEM((groups, 2, 1, lanes), f32)
    grazers = count - NNUT - NPHY
    first, last = call(
        pack_rows,
        (row_message, row_message),
        [HBM, HBM, HBM],
        scratch=[pltpu.VMEM((2, levels, 2, 1, lanes), jnp.int32), pltpu.SemaphoreType.DMA((2, 3))],
        bytes_accessed=8 * groups * lanes,
        limit=2 << 20,
    )(
        in_hbm(tracers.reshape(count * levels, length, 1, lanes)),
        in_hbm(velocity.reshape(2, levels, length, 1, lanes)),
        in_hbm(land_mask.reshape(levels, length, 1, lanes)),
    )
    first, last = first.reshape(2 * groups, lanes), last.reshape(2 * groups, lanes)
    before = lax.ppermute(last, "tx", up(tx))
    after = lax.ppermute(first, "tx", down(tx))

    held, flow, mask = in_vmem(tracers), in_vmem(velocity), in_vmem(land_mask)
    field = pltpu.VMEM(tracers.shape, f32)
    columns = pltpu.VMEM((levels, length, lanes), f32)
    tendency = call(
        ecology,
        field,
        [VMEM] * 4 + [SMEM] * 6,
        scratch=[
            pltpu.VMEM((8 * grazers, 16 * NPHY), jnp.bfloat16),
            pltpu.VMEM((8 * NPHY, 16 * grazers), jnp.bfloat16),
        ],
        flops=40 * cells,
        bytes_accessed=8 * cells,
        limit=2 << 20,
    )(
        held,
        mask,
        in_vmem(sunlight),
        in_vmem(palatable),
        growth_max,
        half_sat,
        light_half,
        graze_max,
        graze_half,
        stoichiometry,
    )
    partial, pack_left, pack_right = call(
        interior,
        (field, columns, columns),
        [VMEM] * 4,
        scratch=[pltpu.VMEM((5, length, lanes), f32)],
        flops=20 * cells,
        bytes_accessed=8 * cells,
        limit=2 << 20,
        input_output_aliases={3: 0},
    )(held, flow, mask, tendency)
    swept, pack_left, pack_right, partial = call(
        border,
        (pltpu.VMEM((count, levels, 16, lanes), f32), columns, columns, field),
        [VMEM] * 5 + [ANY] * 3,
        out_specs=[VMEM] * 3 + [ANY],
        flops=10 * cells,
        bytes_accessed=8 * cells,
        limit=2 << 20,
        input_output_aliases={5: 3, 6: 1, 7: 2},
    )(held, flow, mask, in_vmem(before), in_vmem(after), partial, pack_left, pack_right)
    from_left = lax.ppermute(pack_right, "ty", up(ty))
    from_right = lax.ppermute(pack_left, "ty", down(ty))
    partial, ready = call(
        border_across,
        (field, pltpu.VMEM((PREPARED, levels, length, lanes), f32)),
        [VMEM] * 6,
        flops=10 * cells,
        bytes_accessed=6 * cells,
        limit=2 << 20,
        input_output_aliases={5: 0},
    )(swept, flow, mask, pack_left, pack_right, partial)
    return call(
        finish,
        (field, jax.ShapeDtypeStruct(tracers.shape, f32)),
        [VMEM] * 4,
        out_specs=[VMEM, HBM],
        input_output_aliases={3: 0},
        scratch=[
            pltpu.VMEM((levels, length, lanes), f32),
            pltpu.VMEM((levels, length, lanes), f32),
            pltpu.SemaphoreType.DMA((count // 2,)),
        ],
        flops=4 * cells,
        bytes_accessed=8 * cells,
        limit=2 << 20,
    )(ready, in_vmem(from_left), in_vmem(from_right), partial)[1]


def solution(mesh):
    return jax.shard_map(
        shards,
        mesh=mesh,
        in_specs=(
            P("member", None, "tx", "ty"),
            P(None, None, "tx", "ty"),
            P(None, "tx", "ty"),
            P("tx", "ty"),
            P("member"),
            P("member", None),
            P("member"),
            P("member"),
            P("member"),
            P("member", None),
            P(),
        ),
        out_specs=P("member", None, "tx", "ty"),
        check_vma=False,
    )
```

```python
import jax
import jax.numpy as jnp
from jax import lax
from jax.experimental import pallas as pl
from jax.experimental.pallas import tpu as pltpu
from jax.sharding import PartitionSpec as P


NNUT = 4
NPHY = 26
DEPTH = 12

plankton_mortality = 0.05
grazer_mortality = 0.3
assimilation = 0.3
attenuation = 0.4

VMEM = pl.BlockSpec(memory_space=pltpu.VMEM)
SMEM = pl.BlockSpec(memory_space=pltpu.SMEM)
ANY = pl.BlockSpec(memory_space=pl.ANY)
HBM = pl.BlockSpec(memory_space=pltpu.HBM)


def in_vmem(array):
    return pltpu.with_memory_space_constraint(array, pltpu.VMEM)


def in_hbm(array):
    return pltpu.with_memory_space_constraint(array, pltpu.HBM)


def call(kernel, outs, specs, scratch=(), flops=0, bytes_accessed=0, limit=8 << 20, **more):
    return pl.pallas_call(
        kernel,
        out_shape=outs,
        in_specs=specs,
        scratch_shapes=list(scratch),
        cost_estimate=pl.CostEstimate(flops=flops, bytes_accessed=bytes_accessed, transcendentals=0),
        compiler_params=pltpu.CompilerParams(vmem_limit_bytes=limit),
        **more,
    )


class Deferred:
    def __init__(self, depth):
        self.depth, self.queue = depth, []

    def put(self, ref, index, value):
        self.queue.append((ref, index, value))
        if len(self.queue) > self.depth:
            self.pop()

    def pop(self):
        ref, index, value = self.queue.pop(0)
        ref[index] = value

    def flush(self):
        while self.queue:
            self.pop()


def diet_matrices(palatable, to_grazers, to_plants):
    f32, bf16 = jnp.float32, jnp.bfloat16
    grazers = palatable.shape[0]

    def picks(shape, dim, period):
        index = lax.broadcasted_iota(jnp.int32, shape, dim)
        other = lax.broadcasted_iota(jnp.int32, shape, 1 - dim)
        return ((index % period) // 8 == other).astype(f32).astype(bf16)

    def spread(left, middle, right, transposed):
        dims = (((1,), (1 if transposed else 0,)), ((), ()))
        part = lax.dot_general(left, middle, dims, preferred_element_type=f32).astype(bf16)
        whole = jnp.dot(part, right, preferred_element_type=f32)
        row = lax.broadcasted_iota(jnp.int32, whole.shape, 0) % 8
        col = lax.broadcasted_iota(jnp.int32, whole.shape, 1) % 8
        return jnp.where(row == col, whole, 0.0).astype(bf16)

    eats = palatable[...].astype(f32).astype(bf16)
    rows_z, rows_k = 8 * grazers, 8 * NPHY
    to_grazers[...] = spread(
        picks((rows_z, grazers), 0, rows_z), eats, picks((NPHY, 2 * rows_k), 1, rows_k), False
    )
    to_plants[...] = spread(
        picks((rows_k, NPHY), 0, rows_k), eats, picks((grazers, 2 * rows_z), 1, rows_z), True
    )


def pack_rows(tracers, velocity, mask, first, last, edge, sems):
    count, length = tracers.shape[0], tracers.shape[1]
    levels = mask.shape[0]
    forcing = pl.ds(count, levels)
    copies = []
    for side, (out, rows, row) in enumerate(
        ((first, pl.ds(0, 2), pl.ds(0, 1)), (last, pl.ds(length - 2, 2), pl.ds(length - 1, 1)))
    ):
        copies += [
            pltpu.make_async_copy(tracers.at[:, rows], out.at[pl.ds(0, count)], sems.at[side, 0]),
            pltpu.make_async_copy(
                velocity.at[0, :, row], out.at[forcing, pl.ds(0, 1)], sems.at[side, 1]
            ),
            pltpu.make_async_copy(mask.at[:, row], edge.at[side], sems.at[side, 2]),
        ]
    for copy in copies:
        copy.start()
    for out in (first, last):
        out[count + levels :] = jnp.zeros_like(out[count + levels :])
    for copy in copies:
        copy.wait()
    for side, out in enumerate((first, last)):
        out[forcing, pl.ds(1, 1)] = edge[side].astype(jnp.float32)


def ecology(
    tracers,
    mask,
    sunlight,
    palatable,
    growth_max,
    half_sat,
    light_half,
    graze_max,
    graze_half,
    stoichiometry,
    _,
    tendency,
    to_grazers,
    to_plants,
):
    count, levels, length, lanes = tracers.shape
    grazers = count - NNUT - NPHY
    f32, bf16 = jnp.float32, jnp.bfloat16
    plants = pl.ds(NNUT, NPHY)

    diet_matrices(palatable, to_grazers, to_plants)

    def split(values):
        wide = jnp.concatenate([v.reshape(-1, lanes) for v in values], axis=1)
        high = wide.astype(bf16)
        return jnp.concatenate([high, (wide - high.astype(f32)).astype(bf16)], axis=0)

    def entry(wide, n):
        part = wide[8 * n : 8 * n + 8]
        return jnp.concatenate([part[:, :lanes], part[:, lanes:]], axis=0)

    def level_step(level, carry):
        depth = jnp.exp(jnp.full((8, 128), -attenuation, f32) * (level.astype(f32) + 0.5))[0:1, 0:1]
        for start in range(0, length, 16):
            rows = pl.ds(start, 16)
            halves = (pl.ds(start, 8), pl.ds(start + 8, 8))
            available = jnp.dot(
                to_grazers[...],
                split([tracers[plants, level, half] for half in halves]),
                preferred_element_type=f32,
            )
            wet = mask[level, rows].astype(f32)
            recycled = jnp.zeros((16, lanes), f32)
            rates = []
            later = Deferred(DEPTH)

            def add(t, change):
                later.put(tendency, (t, level, rows), tendency[t, level, rows] + wet * change)

            for z in range(grazers):
                grazer = tracers[NNUT + NPHY + z, level, rows]
                prey = entry(available, z)
                rate = graze_max[z] * grazer / (graze_half[z] + prey)
                ingested = rate * prey
                loss = grazer_mortality * grazer * grazer
                add(NNUT + NPHY + z, assimilation * ingested - loss)
                recycled = recycled + (loss + (1.0 - assimilation) * ingested)
                rates.append(rate)
            pressure = jnp.dot(
                to_plants[...],
                split([jnp.concatenate([r[n : n + 8] for r in rates], axis=0) for n in (0, 8)]),
                preferred_element_type=f32,
            )
            darkness = 1.0 / (sunlight[rows] * depth)
            scarcity = [1.0 / tracers[j, level, rows] for j in range(NNUT)]
            for k in range(NPHY):
                plant = tracers[NNUT + k, level, rows]
                worst = half_sat[0, k] * scarcity[0]
                for j in range(1, NNUT):
                    worst = jnp.maximum(worst, half_sat[j, k] * scarcity[j])
                growth = (growth_max[k] * plant) / (
                    (1.0 + worst) * (1.0 + light_half[k] * darkness)
                )
                recycled = recycled + (plankton_mortality * plant - growth)
                add(NNUT + k, growth - plant * (entry(pressure, k) + plankton_mortality))
            for j in range(NNUT):
                add(j, stoichiometry[j] * recycled)
            later.flush()
        return carry

    lax.fori_loop(0, levels, level_step, 0)


def face_terms(u):
    up, down = jnp.maximum(u, 0.0), jnp.minimum(u, 0.0)
    return (
        up * (-1.0 / 6.0),
        up * (5.0 / 6.0) + down * (1.0 / 3.0),
        up * (1.0 / 3.0) + down * (5.0 / 6.0),
        down * (-1.0 / 6.0),
    )


def stencil(lower, upper):
    a0, b0, d0, e0 = face_terms(lower)
    a1, b1, d1, e1 = face_terms(upper)
    return a0, b0 - a1, 1.0 + (upper - lower) + d0 - b1, e0 - d1, -e1


def row_weights(velocity, mask, level, wet_before, wet_after, flow_after):
    length, lanes = mask.shape[1:]
    rows = lax.broadcasted_iota(jnp.int32, (length, lanes), 0)
    wet = mask[level].astype(jnp.float32)
    wet_up = jnp.where(rows == 0, wet_before, pltpu.roll(wet, 1, 0))
    lower = velocity[0, level] * (wet_up * wet)
    upper = jnp.where(
        rows == length - 1, flow_after * (wet * wet_after), pltpu.roll(lower, length - 1, 0)
    )
    return stencil(lower, upper)


def column_weights(velocity, mask, level, here):
    lanes = mask.shape[2]
    lane = lax.broadcasted_iota(jnp.int32, (8, lanes), 1)
    wet = mask[level, here].astype(jnp.float32)
    lower = jnp.where(lane == 0, 0.0, velocity[1, level, here] * wet * pltpu.roll(wet, 1, 1))
    upper = pltpu.roll(lower, lanes - 1, 1)
    wm2, wm1, w0, wp1, wp2 = stencil(lower, upper)
    return (
        jnp.where(lane < 2, 0.0, wm2),
        jnp.where(lane < 1, 0.0, wm1),
        w0,
        jnp.where(lane > lanes - 2, 0.0, wp1),
        jnp.where(lane > lanes - 3, 0.0, wp2),
    )


def sweep_across(centre, weights):
    wm2, wm1, w0, wp1, wp2 = weights
    lanes = centre.shape[1]
    return (
        w0 * centre
        + (wm1 * pltpu.roll(centre, 1, 1) + wm2 * pltpu.roll(centre, 2, 1))
        + (wp1 * pltpu.roll(centre, lanes - 1, 1) + wp2 * pltpu.roll(centre, lanes - 2, 1))
    )


class Packer:
    def __init__(self, count, velocity, mask, level, here):
        wet = mask[level, here].astype(jnp.float32)
        lane = lax.broadcasted_iota(jnp.int32, wet.shape, 1)
        self.slot = lane // 2
        self.left = self.right = jnp.zeros_like(wet)
        self.add(count, jnp.where(lane < 2, velocity[1, level, here] * wet, wet))

    def add(self, t, value):
        turned = pltpu.roll(value, 2 * t + 2, 1)
        self.right = jnp.where(self.slot == t, turned, self.right)
        self.left = jnp.where(self.slot == t + 1, turned, self.left)


def interior(tracers, velocity, mask, partial, pack_left, pack_right, weights):
    count, levels, length, lanes = tracers.shape
    zero = jnp.zeros((1, lanes), jnp.float32)

    def level_step(level, carry):
        for n, w in enumerate(row_weights(velocity, mask, level, zero, zero, zero)):
            weights[n] = w

        def block_step(block, carry):
            begin = pl.multiple_of(8 * block, 8)
            here = pl.ds(begin, 8)
            wm2, wm1, w0, wp1, wp2 = [weights[n, here] for n in range(5)]
            columns = column_weights(velocity, mask, level, here)
            packer = Packer(count, velocity, mask, level, here)
            later = Deferred(DEPTH)
            for t in range(count):
                at = lambda offset: tracers[t, level, pl.ds(begin + offset, 8)]
                value = (
                    w0 * at(0) + (wm1 * at(-1) + wm2 * at(-2)) + (wp1 * at(1) + wp2 * at(2))
                )
                packer.add(t, value)
                later.put(partial, (t, level, here), sweep_across(value, columns))
            later.flush()
            pack_right[level, here] = packer.right
            pack_left[level, here] = packer.left
            return carry

        for t in range(count):
            partial[t, level, 0:8] = jnp.zeros((8, lanes), jnp.float32)
            partial[t, level, length - 8 : length] = jnp.zeros((8, lanes), jnp.float32)
        return lax.fori_loop(1, length // 8 - 1, block_step, carry)

    lax.fori_loop(0, levels, level_step, 0)


def border(
    tracers, velocity, mask, before, after, partial, left_in, right_in, swept, pack_left, pack_right, through
):
    count, levels, length, lanes = tracers.shape
    row8 = lax.broadcasted_iota(jnp.int32, (8, lanes), 0)

    def level_step(level, carry):
        pick = lambda ref, field: ref[pl.ds(2 * (count * levels + level) + field, 1)]
        weights = row_weights(velocity, mask, level, pick(before, 1), pick(after, 1), pick(after, 0))
        for side, first in enumerate((0, length - 8)):
            here = pl.ds(first, 8)
            wm2, wm1, w0, wp1, wp2 = [w[first : first + 8] for w in weights]
            if side == 0:
                z2, z1 = jnp.where(row8 < 2, wm2, 0.0), jnp.where(row8 < 1, wm1, 0.0)
                wm2, wm1 = jnp.where(row8 < 2, 0.0, wm2), jnp.where(row8 < 1, 0.0, wm1)
            else:
                z2, z1 = jnp.where(row8 > 5, wp2, 0.0), jnp.where(row8 > 6, wp1, 0.0)
                wp2, wp1 = jnp.where(row8 > 5, 0.0, wp2), jnp.where(row8 > 6, 0.0, wp1)
            packer = Packer(count, velocity, mask, level, here)
            later = Deferred(DEPTH)
            for t in range(count):
                centre = tracers[t, level, here]

                def at(offset):
                    if (offset < 0) == (side == 0):
                        return pltpu.roll(centre, -offset % 8, 0)
                    return tracers[t, level, pl.ds(first + offset, 8)]

                group = 2 * (t * levels + level)
                if side == 0:
                    beyond = z2 * before[pl.ds(group, 8)] + z1 * before[pl.ds(group + 1, 8)]
                elif 2 * t * levels < 7:
                    outside = after[pl.ds(group, 8)]
                    beyond = z2 * pltpu.roll(outside, 6, 0) + z1 * pltpu.roll(outside, 7, 0)
                else:
                    beyond = z2 * after[pl.ds(group - 6, 8)] + z1 * after[pl.ds(group - 7, 8)]
                value = (
                    (w0 * centre + beyond) + (wm1 * at(-1) + wm2 * at(-2)) + (wp1 * at(1) + wp2 * at(2))
                )
                later.put(swept, (t, level, pl.ds(8 * side, 8)), value)
                packer.add(t, value)
            later.flush()
            pack_right[level, here] = packer.right
            pack_left[level, here] = packer.left
        return carry

    lax.fori_loop(0, levels, level_step, 0)


PREPARED = 8


def border_across(swept, velocity, mask, my_left, my_right, _, partial, ready):
    count, levels, _, lanes = swept.shape
    length = mask.shape[1]
    place, size = lax.axis_index("ty"), lax.axis_size("ty")
    has_left = jnp.where(place > 0, 1.0, 0.0)
    has_right = jnp.where(place < size - 1, 1.0, 0.0)
    col = lambda value, n: jnp.broadcast_to(value[:, n : n + 1], value.shape)

    def step(index, carry):
        level, side = index // 2, index % 2
        here = pl.ds(pl.multiple_of(side * (length - 8), 8), 8)
        columns = column_weights(velocity, mask, level, here)
        later = Deferred(DEPTH)
        for t in range(count):
            value = swept[t, level, pl.ds(pl.multiple_of(8 * side, 8), 8)]
            later.put(partial, (t, level, here), partial[t, level, here] + sweep_across(value, columns))
        later.flush()
        return carry

    lax.fori_loop(0, 2 * levels, step, 0)

    def prepare(level, carry):
        for block in range(length // 8):
            here = pl.ds(8 * block, 8)
            wet = mask[level, here].astype(jnp.float32)
            flow = velocity[1, level, here]
            opened = flow * wet * pltpu.roll(wet, 1, 1)
            left, right = my_left[level, here], my_right[level, here]
            arrays = (
                col(flow * wet, 0) * has_left,
                col(wet, lanes - 1) * has_right,
                face_terms(col(opened, 1))[0] * has_left,
                face_terms(col(opened, lanes - 1))[3] * has_right,
                pltpu.roll(left, lanes - 2, 1),
                pltpu.roll(left, lanes - 3, 1),
                pltpu.roll(right, lanes - 2, 1),
                pltpu.roll(right, lanes - 1, 1),
            )
            for n, array in enumerate(arrays):
                ready[n, level, here] = array
        return carry

    lax.fori_loop(0, levels, prepare, 0)


def finish(ready, from_left, from_right, _, done, updated, even, odd, sems):
    count, levels, length, lanes = done.shape
    blocks = length // 8
    lane = lax.broadcasted_iota(jnp.int32, (8, lanes), 1)
    is_odd = lane % 2 == 1
    slot_odd = (lane // 2) % 2 == 1
    col = lambda value, n: jnp.broadcast_to(value[:, n : n + 1], value.shape)

    def level_step(level, carry):
        for block in range(blocks):
            here = pl.ds(8 * block, 8)
            open_low, open_high, a1, e127, s0, s1, s127, s126 = (
                ready[n, level, here] for n in range(PREPARED)
            )
            left, right = from_left[level, here], pltpu.roll(from_right[level, here], lanes - 4, 1)
            u0 = open_low * col(left, 2 * count + 1)
            u128 = open_high * col(right, 2 * count - 2)
            a0, b0, d0, e0 = face_terms(u0)
            a128, b128, d128, e128 = face_terms(u128)
            low = jnp.where(is_odd, a1, a0) * left + jnp.where(
                is_odd,
                0.0,
                (b0 - a1) * pltpu.roll(left, lanes - 1, 1) + ((d0 - u0) * s0 + e0 * s1),
            )
            high = jnp.where(
                is_odd,
                (e127 - d128) * pltpu.roll(right, 1, 1) + ((u128 - b128) * s127 - a128 * s126),
                0.0,
            ) - jnp.where(is_odd, e128, e127) * right
            even[level, here] = jnp.where(slot_odd, high, low)
            odd[level, here] = jnp.where(slot_odd, low, high)
        return carry

    lax.fori_loop(0, levels, level_step, 0)
    outer = (lane < 2) | (lane > lanes - 3)
    step = 8 if count % 8 == 0 else 2

    def copy(chunk):
        part = pl.ds(chunk * step, step)
        return pltpu.make_async_copy(done.at[part], updated.at[part], sems.at[chunk])

    def add(chunk, carry):
        start = chunk * step
        turns = [jnp.where(start + n == 0, 0, lanes - 2 * (start + n)) for n in range(step)]
        later = Deferred(2 * DEPTH)
        for level in range(levels):
            for block in range(blocks):
                here = pl.ds(8 * block, 8)
                packs = (even[level, here], odd[level, here])
                for n in range(step):
                    edge = pltpu.roll(packs[n % 2], turns[n], 1)
                    at = (start + n, level, here)
                    later.put(done, at, done[at] + jnp.where(outer, edge, 0.0))
        later.flush()
        copy(chunk).start()
        return carry

    def wait(chunk, carry):
        copy(chunk).wait()
        return carry

    lax.fori_loop(0, count // step, add, 0)
    lax.fori_loop(0, count // step, wait, 0)


def shards(
    tracers,
    velocity,
    land_mask,
    sunlight,
    growth_max,
    half_sat,
    light_half,
    graze_max,
    graze_half,
    palatable,
    stoichiometry,
):
    f32 = jnp.float32
    count, levels, length, lanes = tracers.shape
    tx, ty = lax.axis_size("tx"), lax.axis_size("ty")
    up = lambda n: [(i, (i + 1) % n) for i in range(n)]
    down = lambda n: [((i + 1) % n, i) for i in range(n)]
    cells = count * levels * length * lanes

    assert length % 16 == 0 and count % 2 == 0 and 2 * count + 4 <= lanes
    groups = -(-(count * levels + levels + 1) // 4) * 4
    row_message = pltpu.VMEM((groups, 2, 1, lanes), f32)
    grazers = count - NNUT - NPHY
    first, last = call(
        pack_rows,
        (row_message, row_message),
        [HBM, HBM, HBM],
        scratch=[pltpu.VMEM((2, levels, 1, 1, lanes), jnp.int32), pltpu.SemaphoreType.DMA((2, 3))],
        bytes_accessed=8 * groups * lanes,
        limit=2 << 20,
    )(
        in_hbm(tracers.reshape(count * levels, length, 1, lanes)),
        in_hbm(velocity.reshape(2, levels, length, 1, lanes)),
        in_hbm(land_mask.reshape(levels, length, 1, lanes)),
    )
    first, last = first.reshape(2 * groups, lanes), last.reshape(2 * groups, lanes)
    before = lax.ppermute(last, "tx", up(tx))
    after = lax.ppermute(first, "tx", down(tx))

    held, flow, mask = in_vmem(tracers), in_vmem(velocity), in_vmem(land_mask)
    field = pltpu.VMEM(tracers.shape, f32)
    columns = pltpu.VMEM((levels, length, lanes), f32)
    partial, pack_left, pack_right = call(
        interior,
        (field, columns, columns),
        [VMEM] * 3,
        scratch=[pltpu.VMEM((5, length, lanes), f32)],
        flops=20 * cells,
        bytes_accessed=8 * cells,
        limit=2 << 20,
    )(held, flow, mask)
    partial = call(
        ecology,
        field,
        [VMEM] * 4 + [SMEM] * 6 + [VMEM],
        scratch=[
            pltpu.VMEM((8 * grazers, 16 * NPHY), jnp.bfloat16),
            pltpu.VMEM((8 * NPHY, 16 * grazers), jnp.bfloat16),
        ],
        flops=40 * cells,
        bytes_accessed=8 * cells,
        limit=2 << 20,
        input_output_aliases={10: 0},
    )(
        held,
        mask,
        in_vmem(sunlight),
        in_vmem(palatable),
        growth_max,
        half_sat,
        light_half,
        graze_max,
        graze_half,
        stoichiometry,
        partial,
    )
    swept, pack_left, pack_right, partial = call(
        border,
        (pltpu.VMEM((count, levels, 16, lanes), f32), columns, columns, field),
        [VMEM] * 5 + [ANY] * 3,
        out_specs=[VMEM] * 3 + [ANY],
        flops=10 * cells,
        bytes_accessed=8 * cells,
        limit=2 << 20,
        input_output_aliases={5: 3, 6: 1, 7: 2},
    )(held, flow, mask, in_vmem(before), in_vmem(after), partial, pack_left, pack_right)
    from_left = lax.ppermute(pack_right, "ty", up(ty))
    from_right = lax.ppermute(pack_left, "ty", down(ty))
    partial, ready = call(
        border_across,
        (field, pltpu.VMEM((PREPARED, levels, length, lanes), f32)),
        [VMEM] * 6,
        flops=10 * cells,
        bytes_accessed=6 * cells,
        limit=2 << 20,
        input_output_aliases={5: 0},
    )(swept, flow, mask, pack_left, pack_right, partial)
    return call(
        finish,
        (field, jax.ShapeDtypeStruct(tracers.shape, f32)),
        [VMEM] * 4,
        out_specs=[VMEM, HBM],
        input_output_aliases={3: 0},
        scratch=[
            pltpu.VMEM((levels, length, lanes), f32),
            pltpu.VMEM((levels, length, lanes), f32),
            pltpu.SemaphoreType.DMA((count // 2,)),
        ],
        flops=4 * cells,
        bytes_accessed=8 * cells,
        limit=2 << 20,
    )(ready, in_vmem(from_left), in_vmem(from_right), partial)[1]


def solution(mesh):
    return jax.shard_map(
        shards,
        mesh=mesh,
        in_specs=(
            P("member", None, "tx", "ty"),
            P(None, None, "tx", "ty"),
            P(None, "tx", "ty"),
            P("tx", "ty"),
            P("member"),
            P("member", None),
            P("member"),
            P("member"),
            P("member"),
            P("member", None),
            P(),
        ),
        out_specs=P("member", None, "tx", "ty"),
        check_vma=False,
    )
```

```python
import jax
import jax.numpy as jnp
from jax import lax
from jax.experimental import pallas as pl
from jax.experimental.pallas import tpu as pltpu
from jax.sharding import PartitionSpec as P


NNUT = 4
NPHY = 26
DEPTH = 12

plankton_mortality = 0.05
grazer_mortality = 0.3
assimilation = 0.3
attenuation = 0.4

VMEM = pl.BlockSpec(memory_space=pltpu.VMEM)
SMEM = pl.BlockSpec(memory_space=pltpu.SMEM)
ANY = pl.BlockSpec(memory_space=pl.ANY)
HBM = pl.BlockSpec(memory_space=pltpu.HBM)


def in_vmem(array):
    return pltpu.with_memory_space_constraint(array, pltpu.VMEM)


def in_hbm(array):
    return pltpu.with_memory_space_constraint(array, pltpu.HBM)


def call(kernel, outs, specs, scratch=(), flops=0, bytes_accessed=0, limit=8 << 20, **more):
    return pl.pallas_call(
        kernel,
        out_shape=outs,
        in_specs=specs,
        scratch_shapes=list(scratch),
        cost_estimate=pl.CostEstimate(flops=flops, bytes_accessed=bytes_accessed, transcendentals=0),
        compiler_params=pltpu.CompilerParams(vmem_limit_bytes=limit),
        **more,
    )


class Deferred:
    def __init__(self, depth):
        self.depth, self.queue = depth, []

    def put(self, ref, index, value):
        self.queue.append((ref, index, value))
        if len(self.queue) > self.depth:
            self.pop()

    def pop(self):
        ref, index, value = self.queue.pop(0)
        ref[index] = value

    def flush(self):
        while self.queue:
            self.pop()


def diet_matrices(palatable, to_grazers, to_plants):
    f32, bf16 = jnp.float32, jnp.bfloat16
    grazers = palatable.shape[0]

    def picks(shape, dim, period):
        index = lax.broadcasted_iota(jnp.int32, shape, dim)
        index = jnp.where(index < period, index, index - period)
        other = lax.broadcasted_iota(jnp.int32, shape, 1 - dim)
        return jnp.where((index >> 3) == other, 1.0, 0.0).astype(bf16)

    def spread(left, middle, right, transposed):
        dims = (((1,), (1 if transposed else 0,)), ((), ()))
        part = lax.dot_general(left, middle, dims, preferred_element_type=f32).astype(bf16)
        whole = jnp.dot(part, right, preferred_element_type=f32)
        row = lax.broadcasted_iota(jnp.int32, whole.shape, 0) & 7
        col = lax.broadcasted_iota(jnp.int32, whole.shape, 1) & 7
        return jnp.where(row == col, whole, 0.0).astype(bf16)

    eats = palatable[...].astype(f32).astype(bf16)
    rows_z, rows_k = 8 * grazers, 8 * NPHY
    to_grazers[...] = spread(
        picks((rows_z, grazers), 0, rows_z), eats, picks((NPHY, 2 * rows_k), 1, rows_k), False
    )
    to_plants[...] = spread(
        picks((rows_k, NPHY), 0, rows_k), eats, picks((grazers, 2 * rows_z), 1, rows_z), True
    )


def pack_rows(tracers, velocity, mask, first, last, edge, sems):
    count, length = tracers.shape[0], tracers.shape[1]
    levels = mask.shape[0]
    forcing = pl.ds(count, levels)
    copies = []
    for side, (out, rows, row) in enumerate(
        ((first, pl.ds(0, 2), pl.ds(0, 1)), (last, pl.ds(length - 2, 2), pl.ds(length - 1, 1)))
    ):
        copies += [
            pltpu.make_async_copy(tracers.at[:, rows], out.at[pl.ds(0, count)], sems.at[side, 0]),
            pltpu.make_async_copy(
                velocity.at[0, :, row], out.at[forcing, pl.ds(0, 1)], sems.at[side, 1]
            ),
            pltpu.make_async_copy(mask.at[:, row], edge.at[side], sems.at[side, 2]),
        ]
    for copy in copies:
        copy.start()
    for out in (first, last):
        out[count + levels :] = jnp.zeros_like(out[count + levels :])
    for copy in copies:
        copy.wait()
    for side, out in enumerate((first, last)):
        out[forcing, pl.ds(1, 1)] = edge[side].astype(jnp.float32)


def ecology(
    tracers,
    mask,
    sunlight,
    palatable,
    growth_max,
    half_sat,
    light_half,
    graze_max,
    graze_half,
    stoichiometry,
    _,
    tendency,
    to_grazers,
    to_plants,
):
    count, levels, length, lanes = tracers.shape
    grazers = count - NNUT - NPHY
    f32, bf16 = jnp.float32, jnp.bfloat16
    plants = pl.ds(NNUT, NPHY)

    diet_matrices(palatable, to_grazers, to_plants)

    def split(values):
        wide = jnp.concatenate([v.reshape(-1, lanes) for v in values], axis=1)
        high = wide.astype(bf16)
        return jnp.concatenate([high, (wide - high.astype(f32)).astype(bf16)], axis=0)

    def entry(wide, n):
        part = wide[8 * n : 8 * n + 8]
        return jnp.concatenate([part[:, :lanes], part[:, lanes:]], axis=0)

    def level_step(level, carry):
        depth = jnp.exp(jnp.full((8, 128), -attenuation, f32) * (level.astype(f32) + 0.5))[0:1, 0:1]
        for start in range(0, length, 16):
            rows = pl.ds(start, 16)
            halves = (pl.ds(start, 8), pl.ds(start + 8, 8))
            available = jnp.dot(
                to_grazers[...],
                split([tracers[plants, level, half] for half in halves]),
                preferred_element_type=f32,
            )
            wet = mask[level, rows].astype(f32)
            recycled = jnp.zeros((16, lanes), f32)
            rates = []
            later = Deferred(DEPTH)

            def add(t, change):
                later.put(tendency, (t, level, rows), tendency[t, level, rows] + wet * change)

            for z in range(grazers):
                grazer = tracers[NNUT + NPHY + z, level, rows]
                prey = entry(available, z)
                rate = graze_max[z] * grazer / (graze_half[z] + prey)
                ingested = rate * prey
                loss = grazer_mortality * grazer * grazer
                add(NNUT + NPHY + z, assimilation * ingested - loss)
                recycled = recycled + (loss + (1.0 - assimilation) * ingested)
                rates.append(rate)
            pressure = jnp.dot(
                to_plants[...],
                split([jnp.concatenate([r[n : n + 8] for r in rates], axis=0) for n in (0, 8)]),
                preferred_element_type=f32,
            )
            darkness = 1.0 / (sunlight[rows] * depth)
            scarcity = [1.0 / tracers[j, level, rows] for j in range(NNUT)]
            for k in range(NPHY):
                plant = tracers[NNUT + k, level, rows]
                worst = half_sat[0, k] * scarcity[0]
                for j in range(1, NNUT):
                    worst = jnp.maximum(worst, half_sat[j, k] * scarcity[j])
                growth = (growth_max[k] * plant) / (
                    (1.0 + worst) * (1.0 + light_half[k] * darkness)
                )
                recycled = recycled + (plankton_mortality * plant - growth)
                add(NNUT + k, growth - plant * (entry(pressure, k) + plankton_mortality))
            for j in range(NNUT):
                add(j, stoichiometry[j] * recycled)
            later.flush()
        return carry

    lax.fori_loop(0, levels, level_step, 0)


def face_terms(u):
    up, down = jnp.maximum(u, 0.0), jnp.minimum(u, 0.0)
    return (
        up * (-1.0 / 6.0),
        up * (5.0 / 6.0) + down * (1.0 / 3.0),
        up * (1.0 / 3.0) + down * (5.0 / 6.0),
        down * (-1.0 / 6.0),
    )


def stencil(lower, upper):
    a0, b0, d0, e0 = face_terms(lower)
    a1, b1, d1, e1 = face_terms(upper)
    return a0, b0 - a1, 1.0 + (upper - lower) + d0 - b1, e0 - d1, -e1


def row_weights(velocity, mask, level, wet_before, wet_after, flow_after):
    length, lanes = mask.shape[1:]
    rows = lax.broadcasted_iota(jnp.int32, (length, lanes), 0)
    wet = mask[level].astype(jnp.float32)
    wet_up = jnp.where(rows == 0, wet_before, pltpu.roll(wet, 1, 0))
    lower = velocity[0, level] * (wet_up * wet)
    upper = jnp.where(
        rows == length - 1, flow_after * (wet * wet_after), pltpu.roll(lower, length - 1, 0)
    )
    return stencil(lower, upper)


def column_weights(velocity, mask, level, here):
    lanes = mask.shape[2]
    lane = lax.broadcasted_iota(jnp.int32, (8, lanes), 1)
    wet = mask[level, here].astype(jnp.float32)
    lower = jnp.where(lane == 0, 0.0, velocity[1, level, here] * wet * pltpu.roll(wet, 1, 1))
    upper = pltpu.roll(lower, lanes - 1, 1)
    wm2, wm1, w0, wp1, wp2 = stencil(lower, upper)
    return (
        jnp.where(lane < 2, 0.0, wm2),
        jnp.where(lane < 1, 0.0, wm1),
        w0,
        jnp.where(lane > lanes - 2, 0.0, wp1),
        jnp.where(lane > lanes - 3, 0.0, wp2),
    )


def sweep_across(centre, weights):
    wm2, wm1, w0, wp1, wp2 = weights
    lanes = centre.shape[1]
    return (
        w0 * centre
        + (wm1 * pltpu.roll(centre, 1, 1) + wm2 * pltpu.roll(centre, 2, 1))
        + (wp1 * pltpu.roll(centre, lanes - 1, 1) + wp2 * pltpu.roll(centre, lanes - 2, 1))
    )


def swaps(size):
    return size % 2 == 0


def first_is_right():
    size = lax.axis_size("ty")
    if not swaps(size):
        return True, True
    even = lax.axis_index("ty") % 2 == 0
    return even, jnp.logical_not(even)


def pick(choice, a, b):
    return (a if choice else b) if isinstance(choice, bool) else jnp.where(choice, a, b)


class Packer:
    def __init__(self, count, velocity, mask, level, here):
        wet = mask[level, here].astype(jnp.float32)
        lane = lax.broadcasted_iota(jnp.int32, wet.shape, 1)
        self.slot = lane // 2
        self.left = self.right = jnp.zeros_like(wet)
        self.add(count, jnp.where(lane < 2, velocity[1, level, here] * wet, wet))

    def add(self, t, value):
        turned = pltpu.roll(value, 2 * t + 2, 1)
        self.right = jnp.where(self.slot == t, turned, self.right)
        self.left = jnp.where(self.slot == t + 1, turned, self.left)


def interior(tracers, velocity, mask, partial, pack_first, pack_second, weights):
    count, levels, length, lanes = tracers.shape
    zero = jnp.zeros((1, lanes), jnp.float32)

    def level_step(level, carry):
        for n, w in enumerate(row_weights(velocity, mask, level, zero, zero, zero)):
            weights[n] = w

        def block_step(block, carry):
            begin = pl.multiple_of(8 * block, 8)
            here = pl.ds(begin, 8)
            wm2, wm1, w0, wp1, wp2 = [weights[n, here] for n in range(5)]
            columns = column_weights(velocity, mask, level, here)
            packer = Packer(count, velocity, mask, level, here)
            later = Deferred(DEPTH)
            for t in range(count):
                at = lambda offset: tracers[t, level, pl.ds(begin + offset, 8)]
                value = (
                    w0 * at(0) + (wm1 * at(-1) + wm2 * at(-2)) + (wp1 * at(1) + wp2 * at(2))
                )
                packer.add(t, value)
                later.put(partial, (t, level, here), sweep_across(value, columns))
            later.flush()
            to_right, _ = first_is_right()
            pack_first[level, here] = pick(to_right, packer.right, packer.left)
            pack_second[level, here] = pick(to_right, packer.left, packer.right)
            return carry

        for t in range(count):
            partial[t, level, 0:8] = jnp.zeros((8, lanes), jnp.float32)
            partial[t, level, length - 8 : length] = jnp.zeros((8, lanes), jnp.float32)
        return lax.fori_loop(1, length // 8 - 1, block_step, carry)

    lax.fori_loop(0, levels, level_step, 0)


def border(
    tracers, velocity, mask, before, after, partial, first_in, second_in, swept, pack_first, pack_second, through
):
    count, levels, length, lanes = tracers.shape
    row8 = lax.broadcasted_iota(jnp.int32, (8, lanes), 0)

    def level_step(level, carry):
        row = lambda ref, field: ref[pl.ds(2 * (count * levels + level) + field, 1)]
        weights = row_weights(velocity, mask, level, row(before, 1), row(after, 1), row(after, 0))
        for side, first in enumerate((0, length - 8)):
            here = pl.ds(first, 8)
            wm2, wm1, w0, wp1, wp2 = [w[first : first + 8] for w in weights]
            if side == 0:
                z2, z1 = jnp.where(row8 < 2, wm2, 0.0), jnp.where(row8 < 1, wm1, 0.0)
                wm2, wm1 = jnp.where(row8 < 2, 0.0, wm2), jnp.where(row8 < 1, 0.0, wm1)
            else:
                z2, z1 = jnp.where(row8 > 5, wp2, 0.0), jnp.where(row8 > 6, wp1, 0.0)
                wp2, wp1 = jnp.where(row8 > 5, 0.0, wp2), jnp.where(row8 > 6, 0.0, wp1)
            packer = Packer(count, velocity, mask, level, here)
            later = Deferred(DEPTH)
            for t in range(count):
                centre = tracers[t, level, here]

                def at(offset):
                    if (offset < 0) == (side == 0):
                        return pltpu.roll(centre, -offset % 8, 0)
                    return tracers[t, level, pl.ds(first + offset, 8)]

                group = 2 * (t * levels + level)
                if side == 0:
                    beyond = z2 * before[pl.ds(group, 8)] + z1 * before[pl.ds(group + 1, 8)]
                elif 2 * t * levels < 7:
                    outside = after[pl.ds(group, 8)]
                    beyond = z2 * pltpu.roll(outside, 6, 0) + z1 * pltpu.roll(outside, 7, 0)
                else:
                    beyond = z2 * after[pl.ds(group - 6, 8)] + z1 * after[pl.ds(group - 7, 8)]
                value = (
                    (w0 * centre + beyond) + (wm1 * at(-1) + wm2 * at(-2)) + (wp1 * at(1) + wp2 * at(2))
                )
                later.put(swept, (t, level, pl.ds(8 * side, 8)), value)
                packer.add(t, value)
            later.flush()
            to_right, _ = first_is_right()
            pack_first[level, here] = pick(to_right, packer.right, packer.left)
            pack_second[level, here] = pick(to_right, packer.left, packer.right)
        return carry

    lax.fori_loop(0, levels, level_step, 0)


PREPARED = 8


def border_across(swept, velocity, mask, my_first, my_second, _, partial, ready):
    count, levels, _, lanes = swept.shape
    length = mask.shape[1]
    place, size = lax.axis_index("ty"), lax.axis_size("ty")
    has_left = jnp.where(place > 0, 1.0, 0.0)
    has_right = jnp.where(place < size - 1, 1.0, 0.0)
    col = lambda value, n: jnp.broadcast_to(value[:, n : n + 1], value.shape)

    def step(index, carry):
        level, side = index // 2, index % 2
        here = pl.ds(pl.multiple_of(side * (length - 8), 8), 8)
        columns = column_weights(velocity, mask, level, here)
        later = Deferred(DEPTH)
        for t in range(count):
            value = swept[t, level, pl.ds(pl.multiple_of(8 * side, 8), 8)]
            later.put(partial, (t, level, here), partial[t, level, here] + sweep_across(value, columns))
        later.flush()
        return carry

    lax.fori_loop(0, 2 * levels, step, 0)

    def prepare(level, carry):
        for block in range(length // 8):
            here = pl.ds(8 * block, 8)
            wet = mask[level, here].astype(jnp.float32)
            flow = velocity[1, level, here]
            opened = flow * wet * pltpu.roll(wet, 1, 1)
            to_right, _ = first_is_right()
            first, second = my_first[level, here], my_second[level, here]
            left, right = pick(to_right, second, first), pick(to_right, first, second)
            arrays = (
                col(flow * wet, 0) * has_left,
                col(wet, lanes - 1) * has_right,
                face_terms(col(opened, 1))[0] * has_left,
                face_terms(col(opened, lanes - 1))[3] * has_right,
                pltpu.roll(left, lanes - 2, 1),
                pltpu.roll(left, lanes - 3, 1),
                pltpu.roll(right, lanes - 2, 1),
                pltpu.roll(right, lanes - 1, 1),
            )
            for n, array in enumerate(arrays):
                ready[n, level, here] = array
        return carry

    lax.fori_loop(0, levels, prepare, 0)


def finish(ready, first, second, _, done, updated, even, odd, sems):
    count, levels, length, lanes = done.shape
    blocks = length // 8
    lane = lax.broadcasted_iota(jnp.int32, (8, lanes), 1)
    is_odd = lane % 2 == 1
    slot_odd = (lane // 2) % 2 == 1
    col = lambda value, n: jnp.broadcast_to(value[:, n : n + 1], value.shape)

    def level_step(level, carry):
        for block in range(blocks):
            here = pl.ds(8 * block, 8)
            open_low, open_high, a1, e127, s0, s1, s127, s126 = (
                ready[n, level, here] for n in range(PREPARED)
            )
            _, of_left = first_is_right()
            one, two = first[level, here], second[level, here]
            left = pick(of_left, one, two)
            right = pltpu.roll(pick(of_left, two, one), lanes - 4, 1)
            u0 = open_low * col(left, 2 * count + 1)
            u128 = open_high * col(right, 2 * count - 2)
            a0, b0, d0, e0 = face_terms(u0)
            a128, b128, d128, e128 = face_terms(u128)
            low = jnp.where(is_odd, a1, a0) * left + jnp.where(
                is_odd,
                0.0,
                (b0 - a1) * pltpu.roll(left, lanes - 1, 1) + ((d0 - u0) * s0 + e0 * s1),
            )
            high = jnp.where(
                is_odd,
                (e127 - d128) * pltpu.roll(right, 1, 1) + ((u128 - b128) * s127 - a128 * s126),
                0.0,
            ) - jnp.where(is_odd, e128, e127) * right
            even[level, here] = jnp.where(slot_odd, high, low)
            odd[level, here] = jnp.where(slot_odd, low, high)
        return carry

    lax.fori_loop(0, levels, level_step, 0)
    outer = (lane < 2) | (lane > lanes - 3)
    step = 8 if count % 8 == 0 else 2

    def copy(chunk):
        part = pl.ds(chunk * step, step)
        return pltpu.make_async_copy(done.at[part], updated.at[part], sems.at[chunk])

    def add(chunk, carry):
        start = chunk * step
        turns = [jnp.where(start + n == 0, 0, lanes - 2 * (start + n)) for n in range(step)]
        later = Deferred(2 * DEPTH)
        for level in range(levels):
            for block in range(blocks):
                here = pl.ds(8 * block, 8)
                packs = (even[level, here], odd[level, here])
                for n in range(step):
                    edge = pltpu.roll(packs[n % 2], turns[n], 1)
                    at = (start + n, level, here)
                    later.put(done, at, done[at] + jnp.where(outer, edge, 0.0))
        later.flush()
        copy(chunk).start()
        return carry

    def wait(chunk, carry):
        copy(chunk).wait()
        return carry

    lax.fori_loop(0, count // step, add, 0)
    lax.fori_loop(0, count // step, wait, 0)


def shards(
    tracers,
    velocity,
    land_mask,
    sunlight,
    growth_max,
    half_sat,
    light_half,
    graze_max,
    graze_half,
    palatable,
    stoichiometry,
):
    f32 = jnp.float32
    count, levels, length, lanes = tracers.shape
    tx, ty = lax.axis_size("tx"), lax.axis_size("ty")
    up = lambda n: [(i, (i + 1) % n) for i in range(n)]
    down = lambda n: [((i + 1) % n, i) for i in range(n)]
    cells = count * levels * length * lanes

    assert length % 16 == 0 and count % 2 == 0 and 2 * count + 4 <= lanes
    groups = -(-(count * levels + levels + 1) // 4) * 4
    row_message = pltpu.VMEM((groups, 2, 1, lanes), f32)
    grazers = count - NNUT - NPHY
    first, last = call(
        pack_rows,
        (row_message, row_message),
        [HBM, HBM, HBM],
        scratch=[pltpu.VMEM((2, levels, 1, 1, lanes), jnp.int32), pltpu.SemaphoreType.DMA((2, 3))],
        bytes_accessed=8 * groups * lanes,
        limit=2 << 20,
    )(
        in_hbm(tracers.reshape(count * levels, length, 1, lanes)),
        in_hbm(velocity.reshape(2, levels, length, 1, lanes)),
        in_hbm(land_mask.reshape(levels, length, 1, lanes)),
    )
    first, last = first.reshape(2 * groups, lanes), last.reshape(2 * groups, lanes)
    before = lax.ppermute(last, "tx", up(tx))
    after = lax.ppermute(first, "tx", down(tx))

    held, flow, mask = in_vmem(tracers), in_vmem(velocity), in_vmem(land_mask)
    field = pltpu.VMEM(tracers.shape, f32)
    columns = pltpu.VMEM((levels, length, lanes), f32)
    partial, pack_first, pack_second = call(
        interior,
        (field, columns, columns),
        [VMEM] * 3,
        scratch=[pltpu.VMEM((5, length, lanes), f32)],
        flops=20 * cells,
        bytes_accessed=8 * cells,
        limit=2 << 20,
    )(held, flow, mask)
    partial = call(
        ecology,
        field,
        [VMEM] * 4 + [SMEM] * 6 + [VMEM],
        scratch=[
            pltpu.VMEM((8 * grazers, 16 * NPHY), jnp.bfloat16),
            pltpu.VMEM((8 * NPHY, 16 * grazers), jnp.bfloat16),
        ],
        flops=40 * cells,
        bytes_accessed=8 * cells,
        limit=2 << 20,
        input_output_aliases={10: 0},
    )(
        held,
        mask,
        in_vmem(sunlight),
        in_vmem(palatable),
        growth_max,
        half_sat,
        light_half,
        graze_max,
        graze_half,
        stoichiometry,
        partial,
    )
    swept, pack_first, pack_second, partial = call(
        border,
        (pltpu.VMEM((count, levels, 16, lanes), f32), columns, columns, field),
        [VMEM] * 5 + [ANY] * 3,
        out_specs=[VMEM] * 3 + [ANY],
        flops=10 * cells,
        bytes_accessed=8 * cells,
        limit=2 << 20,
        input_output_aliases={5: 3, 6: 1, 7: 2},
    )(held, flow, mask, in_vmem(before), in_vmem(after), partial, pack_first, pack_second)
    pair = lambda n, odd: [p for i in range(odd, n, 2) for p in ((i, (i + 1) % n), ((i + 1) % n, i))]
    turns = (pair(ty, 0), pair(ty, 1)) if swaps(ty) else (up(ty), down(ty))
    from_first = lax.ppermute(pack_first, "ty", turns[0])
    from_second = lax.ppermute(pack_second, "ty", turns[1])
    partial, ready = call(
        border_across,
        (field, pltpu.VMEM((PREPARED, levels, length, lanes), f32)),
        [VMEM] * 6,
        flops=10 * cells,
        bytes_accessed=6 * cells,
        limit=2 << 20,
        input_output_aliases={5: 0},
    )(swept, flow, mask, pack_first, pack_second, partial)
    return call(
        finish,
        (field, jax.ShapeDtypeStruct(tracers.shape, f32)),
        [VMEM] * 4,
        out_specs=[VMEM, HBM],
        input_output_aliases={3: 0},
        scratch=[
            pltpu.VMEM((levels, length, lanes), f32),
            pltpu.VMEM((levels, length, lanes), f32),
            pltpu.SemaphoreType.DMA((count // 2,)),
        ],
        flops=4 * cells,
        bytes_accessed=8 * cells,
        limit=2 << 20,
    )(ready, in_vmem(from_first), in_vmem(from_second), partial)[1]


def solution(mesh):
    return jax.shard_map(
        shards,
        mesh=mesh,
        in_specs=(
            P("member", None, "tx", "ty"),
            P(None, None, "tx", "ty"),
            P(None, "tx", "ty"),
            P("tx", "ty"),
            P("member"),
            P("member", None),
            P("member"),
            P("member"),
            P("member"),
            P("member", None),
            P(),
        ),
        out_specs=P("member", None, "tx", "ty"),
        check_vma=False,
    )
```

```python
import jax
import jax.numpy as jnp
from jax import lax
from jax.experimental import pallas as pl
from jax.experimental.pallas import tpu as pltpu
from jax.sharding import PartitionSpec as P


NNUT = 4
NPHY = 26
DEPTH = 12

plankton_mortality = 0.05
grazer_mortality = 0.3
assimilation = 0.3
attenuation = 0.4

VMEM = pl.BlockSpec(memory_space=pltpu.VMEM)
SMEM = pl.BlockSpec(memory_space=pltpu.SMEM)
ANY = pl.BlockSpec(memory_space=pl.ANY)
HBM = pl.BlockSpec(memory_space=pltpu.HBM)


def in_vmem(array):
    return pltpu.with_memory_space_constraint(array, pltpu.VMEM)


def in_hbm(array):
    return pltpu.with_memory_space_constraint(array, pltpu.HBM)


def call(kernel, outs, specs, scratch=(), flops=0, bytes_accessed=0, limit=8 << 20, **more):
    return pl.pallas_call(
        kernel,
        out_shape=outs,
        in_specs=specs,
        scratch_shapes=list(scratch),
        cost_estimate=pl.CostEstimate(flops=flops, bytes_accessed=bytes_accessed, transcendentals=0),
        compiler_params=pltpu.CompilerParams(vmem_limit_bytes=limit),
        **more,
    )


class Deferred:
    def __init__(self, depth):
        self.depth, self.queue = depth, []

    def put(self, ref, index, value):
        self.queue.append((ref, index, value))
        if len(self.queue) > self.depth:
            self.pop()

    def pop(self):
        ref, index, value = self.queue.pop(0)
        ref[index] = value

    def flush(self):
        while self.queue:
            self.pop()


def diet_matrices(palatable, to_grazers, to_plants):
    f32, bf16 = jnp.float32, jnp.bfloat16
    grazers = palatable.shape[0]

    def picks(shape, dim, period):
        index = lax.broadcasted_iota(jnp.int32, shape, dim)
        index = jnp.where(index < period, index, index - period)
        other = lax.broadcasted_iota(jnp.int32, shape, 1 - dim)
        return jnp.where((index >> 3) == other, 1.0, 0.0).astype(bf16)

    def spread(left, middle, right, transposed):
        dims = (((1,), (1 if transposed else 0,)), ((), ()))
        part = lax.dot_general(left, middle, dims, preferred_element_type=f32).astype(bf16)
        whole = jnp.dot(part, right, preferred_element_type=f32)
        row = lax.broadcasted_iota(jnp.int32, whole.shape, 0) & 7
        col = lax.broadcasted_iota(jnp.int32, whole.shape, 1) & 7
        return jnp.where(row == col, whole, 0.0).astype(bf16)

    eats = palatable[...].astype(f32).astype(bf16)
    rows_z, rows_k = 8 * grazers, 8 * NPHY
    to_grazers[...] = spread(
        picks((rows_z, grazers), 0, rows_z), eats, picks((NPHY, 2 * rows_k), 1, rows_k), False
    )
    to_plants[...] = spread(
        picks((rows_k, NPHY), 0, rows_k), eats, picks((grazers, 2 * rows_z), 1, rows_z), True
    )


def pack_rows(tracers, velocity, mask, first, last, edge, sems):
    count, length = tracers.shape[0], tracers.shape[1]
    levels = mask.shape[0]
    forcing = pl.ds(count, levels)
    copies = []
    for side, (out, rows, row) in enumerate(
        ((first, pl.ds(0, 2), pl.ds(0, 1)), (last, pl.ds(length - 2, 2), pl.ds(length - 1, 1)))
    ):
        copies += [
            pltpu.make_async_copy(tracers.at[:, rows], out.at[pl.ds(0, count)], sems.at[side, 0]),
            pltpu.make_async_copy(
                velocity.at[0, :, row], out.at[forcing, pl.ds(0, 1)], sems.at[side, 1]
            ),
            pltpu.make_async_copy(mask.at[:, row], edge.at[side], sems.at[side, 2]),
        ]
    for copy in copies:
        copy.start()
    for out in (first, last):
        out[count + levels :] = jnp.zeros_like(out[count + levels :])
    for copy in copies:
        copy.wait()
    for side, out in enumerate((first, last)):
        out[forcing, pl.ds(1, 1)] = edge[side].astype(jnp.float32)


def ecology(
    tracers,
    mask,
    sunlight,
    palatable,
    growth_max,
    half_sat,
    light_half,
    graze_max,
    graze_half,
    stoichiometry,
    _,
    tendency,
    to_grazers,
    to_plants,
):
    count, levels, length, lanes = tracers.shape
    grazers = count - NNUT - NPHY
    f32, bf16 = jnp.float32, jnp.bfloat16
    plants = pl.ds(NNUT, NPHY)

    diet_matrices(palatable, to_grazers, to_plants)

    def split(values):
        wide = jnp.concatenate([v.reshape(-1, lanes) for v in values], axis=1)
        high = wide.astype(bf16)
        return jnp.concatenate([high, (wide - high.astype(f32)).astype(bf16)], axis=0)

    def entry(wide, n):
        part = wide[8 * n : 8 * n + 8]
        return jnp.concatenate([part[:, :lanes], part[:, lanes:]], axis=0)

    def level_step(level, carry):
        depth = jnp.exp(jnp.full((8, 128), -attenuation, f32) * (level.astype(f32) + 0.5))[0:1, 0:1]
        for start in range(0, length, 16):
            rows = pl.ds(start, 16)
            halves = (pl.ds(start, 8), pl.ds(start + 8, 8))
            available = jnp.dot(
                to_grazers[...],
                split([tracers[plants, level, half] for half in halves]),
                preferred_element_type=f32,
            )
            wet = mask[level, rows].astype(f32)
            recycled = jnp.zeros((16, lanes), f32)
            rates = []
            later = Deferred(DEPTH)

            def add(t, change):
                later.put(tendency, (t, level, rows), tendency[t, level, rows] + wet * change)

            for z in range(grazers):
                grazer = tracers[NNUT + NPHY + z, level, rows]
                prey = entry(available, z)
                rate = graze_max[z] * grazer / (graze_half[z] + prey)
                ingested = rate * prey
                loss = grazer_mortality * grazer * grazer
                add(NNUT + NPHY + z, assimilation * ingested - loss)
                recycled = recycled + (loss + (1.0 - assimilation) * ingested)
                rates.append(rate)
            pressure = jnp.dot(
                to_plants[...],
                split([jnp.concatenate([r[n : n + 8] for r in rates], axis=0) for n in (0, 8)]),
                preferred_element_type=f32,
            )
            darkness = 1.0 / (sunlight[rows] * depth)
            scarcity = [1.0 / tracers[j, level, rows] for j in range(NNUT)]
            for k in range(NPHY):
                plant = tracers[NNUT + k, level, rows]
                worst = half_sat[0, k] * scarcity[0]
                for j in range(1, NNUT):
                    worst = jnp.maximum(worst, half_sat[j, k] * scarcity[j])
                growth = (growth_max[k] * plant) / (
                    (1.0 + worst) * (1.0 + light_half[k] * darkness)
                )
                recycled = recycled + (plankton_mortality * plant - growth)
                add(NNUT + k, growth - plant * (entry(pressure, k) + plankton_mortality))
            for j in range(NNUT):
                add(j, stoichiometry[j] * recycled)
            later.flush()
        return carry

    lax.fori_loop(0, levels, level_step, 0)


def face_terms(u):
    up, down = jnp.maximum(u, 0.0), jnp.minimum(u, 0.0)
    return (
        up * (-1.0 / 6.0),
        up * (5.0 / 6.0) + down * (1.0 / 3.0),
        up * (1.0 / 3.0) + down * (5.0 / 6.0),
        down * (-1.0 / 6.0),
    )


def stencil(lower, upper):
    a0, b0, d0, e0 = face_terms(lower)
    a1, b1, d1, e1 = face_terms(upper)
    return a0, b0 - a1, 1.0 + (upper - lower) + d0 - b1, e0 - d1, -e1


def row_weights(velocity, mask, level, wet_before, wet_after, flow_after):
    length, lanes = mask.shape[1:]
    rows = lax.broadcasted_iota(jnp.int32, (length, lanes), 0)
    wet = mask[level].astype(jnp.float32)
    wet_up = jnp.where(rows == 0, wet_before, pltpu.roll(wet, 1, 0))
    lower = velocity[0, level] * (wet_up * wet)
    upper = jnp.where(
        rows == length - 1, flow_after * (wet * wet_after), pltpu.roll(lower, length - 1, 0)
    )
    return stencil(lower, upper)


def column_weights(velocity, mask, level, here):
    lanes = mask.shape[2]
    lane = lax.broadcasted_iota(jnp.int32, (8, lanes), 1)
    wet = mask[level, here].astype(jnp.float32)
    lower = jnp.where(lane == 0, 0.0, velocity[1, level, here] * wet * pltpu.roll(wet, 1, 1))
    upper = pltpu.roll(lower, lanes - 1, 1)
    wm2, wm1, w0, wp1, wp2 = stencil(lower, upper)
    return (
        jnp.where(lane < 2, 0.0, wm2),
        jnp.where(lane < 1, 0.0, wm1),
        w0,
        jnp.where(lane > lanes - 2, 0.0, wp1),
        jnp.where(lane > lanes - 3, 0.0, wp2),
    )


def sweep_across(centre, weights):
    wm2, wm1, w0, wp1, wp2 = weights
    lanes = centre.shape[1]
    return (
        w0 * centre
        + (wm1 * pltpu.roll(centre, 1, 1) + wm2 * pltpu.roll(centre, 2, 1))
        + (wp1 * pltpu.roll(centre, lanes - 1, 1) + wp2 * pltpu.roll(centre, lanes - 2, 1))
    )


def swaps(size):
    return size % 2 == 0


def first_is_right():
    size = lax.axis_size("ty")
    if not swaps(size):
        return True, True
    even = lax.axis_index("ty") % 2 == 0
    return even, jnp.logical_not(even)


def pick(choice, a, b):
    return (a if choice else b) if isinstance(choice, bool) else jnp.where(choice, a, b)


class Packer:
    def __init__(self, count, velocity, mask, level, here):
        wet = mask[level, here].astype(jnp.float32)
        lane = lax.broadcasted_iota(jnp.int32, wet.shape, 1)
        self.slot = lane // 2
        self.left = self.right = jnp.zeros_like(wet)
        self.add(count, jnp.where(lane < 2, velocity[1, level, here] * wet, wet))

    def add(self, t, value):
        turned = pltpu.roll(value, 2 * t + 2, 1)
        self.right = jnp.where(self.slot == t, turned, self.right)
        self.left = jnp.where(self.slot == t + 1, turned, self.left)


def interior(
    tracers, velocity, mask, partial, pack_first, pack_second, columns, weights
):
    count, levels, length, lanes = tracers.shape
    zero = jnp.zeros((1, lanes), jnp.float32)
    for level in range(levels):
        for n, w in enumerate(row_weights(velocity, mask, level, zero, zero, zero)):
            weights[n, level] = w
        for block in range(length // 8):
            here = pl.ds(8 * block, 8)
            for n, w in enumerate(column_weights(velocity, mask, level, here)):
                columns[n, level, here] = w
    to_right, _ = first_is_right()
    blocks = length // 8 - 2

    def step(index, carry):
        level = index // blocks
        begin = pl.multiple_of(8 * (1 + index % blocks), 8)
        here = pl.ds(begin, 8)
        wm2, wm1, w0, wp1, wp2 = [weights[n, level, here] for n in range(5)]
        sideways = [columns[n, level, here] for n in range(5)]
        packer = Packer(count, velocity, mask, level, here)
        later = Deferred(DEPTH)
        for t in range(count):
            at = lambda offset: tracers[t, level, pl.ds(begin + offset, 8)]
            value = w0 * at(0) + (wm1 * at(-1) + wm2 * at(-2)) + (wp1 * at(1) + wp2 * at(2))
            packer.add(t, value)
            later.put(partial, (t, level, here), sweep_across(value, sideways))
        later.flush()
        pack_first[level, here] = pick(to_right, packer.right, packer.left)
        pack_second[level, here] = pick(to_right, packer.left, packer.right)
        return carry

    def clear(level, carry):
        for t in range(count):
            partial[t, level, 0:8] = jnp.zeros((8, lanes), jnp.float32)
            partial[t, level, length - 8 : length] = jnp.zeros((8, lanes), jnp.float32)
        return carry

    lax.fori_loop(0, levels, clear, 0)
    lax.fori_loop(0, levels * blocks, step, 0)


def border(
    tracers, velocity, mask, before, after, partial, first_in, second_in, swept, pack_first, pack_second, through, weights
):
    count, levels, length, lanes = tracers.shape
    row8 = lax.broadcasted_iota(jnp.int32, (8, lanes), 0)

    for level in range(levels):
        row = lambda ref, field: ref[pl.ds(2 * (count * levels + level) + field, 1)]
        for n, w in enumerate(
            row_weights(velocity, mask, level, row(before, 1), row(after, 1), row(after, 0))
        ):
            weights[n, level] = w

    def level_step(level, carry):
        for side, first in enumerate((0, length - 8)):
            here = pl.ds(first, 8)
            wm2, wm1, w0, wp1, wp2 = [weights[n, level, here] for n in range(5)]
            if side == 0:
                z2, z1 = jnp.where(row8 < 2, wm2, 0.0), jnp.where(row8 < 1, wm1, 0.0)
                wm2, wm1 = jnp.where(row8 < 2, 0.0, wm2), jnp.where(row8 < 1, 0.0, wm1)
            else:
                z2, z1 = jnp.where(row8 > 5, wp2, 0.0), jnp.where(row8 > 6, wp1, 0.0)
                wp2, wp1 = jnp.where(row8 > 5, 0.0, wp2), jnp.where(row8 > 6, 0.0, wp1)
            packer = Packer(count, velocity, mask, level, here)
            later = Deferred(DEPTH)
            for t in range(count):
                centre = tracers[t, level, here]

                def at(offset):
                    if (offset < 0) == (side == 0):
                        return pltpu.roll(centre, -offset % 8, 0)
                    return tracers[t, level, pl.ds(first + offset, 8)]

                group = 2 * (t * levels + level)
                if side == 0:
                    beyond = z2 * before[pl.ds(group, 8)] + z1 * before[pl.ds(group + 1, 8)]
                elif 2 * t * levels < 7:
                    outside = after[pl.ds(group, 8)]
                    beyond = z2 * pltpu.roll(outside, 6, 0) + z1 * pltpu.roll(outside, 7, 0)
                else:
                    beyond = z2 * after[pl.ds(group - 6, 8)] + z1 * after[pl.ds(group - 7, 8)]
                value = (
                    (w0 * centre + beyond) + (wm1 * at(-1) + wm2 * at(-2)) + (wp1 * at(1) + wp2 * at(2))
                )
                later.put(swept, (t, level, pl.ds(8 * side, 8)), value)
                packer.add(t, value)
            later.flush()
            to_right, _ = first_is_right()
            pack_first[level, here] = pick(to_right, packer.right, packer.left)
            pack_second[level, here] = pick(to_right, packer.left, packer.right)
        return carry

    lax.fori_loop(0, levels, level_step, 0)


PREPARED = 8


def border_across(swept, velocity, mask, columns, my_first, my_second, _, partial, ready):
    count, levels, _, lanes = swept.shape
    length = mask.shape[1]
    place, size = lax.axis_index("ty"), lax.axis_size("ty")
    has_left = jnp.where(place > 0, 1.0, 0.0)
    has_right = jnp.where(place < size - 1, 1.0, 0.0)
    col = lambda value, n: jnp.broadcast_to(value[:, n : n + 1], value.shape)

    def step(index, carry):
        level, side = index // 2, index % 2
        here = pl.ds(pl.multiple_of(side * (length - 8), 8), 8)
        sideways = [columns[n, level, here] for n in range(5)]
        later = Deferred(DEPTH)
        for t in range(count):
            value = swept[t, level, pl.ds(pl.multiple_of(8 * side, 8), 8)]
            later.put(partial, (t, level, here), partial[t, level, here] + sweep_across(value, sideways))
        later.flush()
        return carry

    lax.fori_loop(0, 2 * levels, step, 0)

    def prepare(level, carry):
        for block in range(length // 8):
            here = pl.ds(8 * block, 8)
            wet = mask[level, here].astype(jnp.float32)
            flow = velocity[1, level, here]
            opened = flow * wet * pltpu.roll(wet, 1, 1)
            to_right, _ = first_is_right()
            first, second = my_first[level, here], my_second[level, here]
            left, right = pick(to_right, second, first), pick(to_right, first, second)
            arrays = (
                col(flow * wet, 0) * has_left,
                col(wet, lanes - 1) * has_right,
                face_terms(col(opened, 1))[0] * has_left,
                face_terms(col(opened, lanes - 1))[3] * has_right,
                pltpu.roll(left, lanes - 2, 1),
                pltpu.roll(left, lanes - 3, 1),
                pltpu.roll(right, lanes - 2, 1),
                pltpu.roll(right, lanes - 1, 1),
            )
            for n, array in enumerate(arrays):
                ready[n, level, here] = array
        return carry

    for level in range(levels):
        prepare(level, 0)


def finish(ready, first, second, _, done, updated, even, odd, sems):
    count, levels, length, lanes = done.shape
    blocks = length // 8
    lane = lax.broadcasted_iota(jnp.int32, (8, lanes), 1)
    is_odd = lane % 2 == 1
    slot_odd = (lane // 2) % 2 == 1
    col = lambda value, n: jnp.broadcast_to(value[:, n : n + 1], value.shape)

    def level_step(level, carry):
        for block in range(blocks):
            here = pl.ds(8 * block, 8)
            open_low, open_high, a1, e127, s0, s1, s127, s126 = (
                ready[n, level, here] for n in range(PREPARED)
            )
            _, of_left = first_is_right()
            one, two = first[level, here], second[level, here]
            left = pick(of_left, one, two)
            right = pltpu.roll(pick(of_left, two, one), lanes - 4, 1)
            u0 = open_low * col(left, 2 * count + 1)
            u128 = open_high * col(right, 2 * count - 2)
            a0, b0, d0, e0 = face_terms(u0)
            a128, b128, d128, e128 = face_terms(u128)
            low = jnp.where(is_odd, a1, a0) * left + jnp.where(
                is_odd,
                0.0,
                (b0 - a1) * pltpu.roll(left, lanes - 1, 1) + ((d0 - u0) * s0 + e0 * s1),
            )
            high = jnp.where(
                is_odd,
                (e127 - d128) * pltpu.roll(right, 1, 1) + ((u128 - b128) * s127 - a128 * s126),
                0.0,
            ) - jnp.where(is_odd, e128, e127) * right
            even[level, here] = jnp.where(slot_odd, high, low)
            odd[level, here] = jnp.where(slot_odd, low, high)
        return carry

    for level in range(levels):
        level_step(level, 0)
    outer = (lane < 2) | (lane > lanes - 3)
    step = 8 if count % 8 == 0 else 2

    def copy(chunk):
        part = pl.ds(chunk * step, step)
        return pltpu.make_async_copy(done.at[part], updated.at[part], sems.at[chunk])

    def add(chunk, carry):
        start = chunk * step
        turns = [jnp.where(start + n == 0, 0, lanes - 2 * (start + n)) for n in range(step)]
        later = Deferred(2 * DEPTH)
        for n in range(step):
            for level in range(levels):
                for block in range(blocks):
                    here = pl.ds(8 * block, 8)
                    edge = pltpu.roll((even, odd)[n % 2][level, here], turns[n], 1)
                    at = (start + n, level, here)
                    later.put(done, at, done[at] + jnp.where(outer, edge, 0.0))
        later.flush()
        copy(chunk).start()
        return carry

    def wait(chunk, carry):
        copy(chunk).wait()
        return carry

    lax.fori_loop(0, count // step, add, 0)
    lax.fori_loop(0, count // step, wait, 0)


def shards(
    tracers,
    velocity,
    land_mask,
    sunlight,
    growth_max,
    half_sat,
    light_half,
    graze_max,
    graze_half,
    palatable,
    stoichiometry,
):
    f32 = jnp.float32
    count, levels, length, lanes = tracers.shape
    tx, ty = lax.axis_size("tx"), lax.axis_size("ty")
    up = lambda n: [(i, (i + 1) % n) for i in range(n)]
    down = lambda n: [((i + 1) % n, i) for i in range(n)]
    cells = count * levels * length * lanes

    assert length % 16 == 0 and count % 2 == 0 and 2 * count + 4 <= lanes
    groups = -(-(count * levels + levels + 1) // 4) * 4
    row_message = pltpu.VMEM((groups, 2, 1, lanes), f32)
    grazers = count - NNUT - NPHY
    first, last = call(
        pack_rows,
        (row_message, row_message),
        [HBM, HBM, HBM],
        scratch=[pltpu.VMEM((2, levels, 1, 1, lanes), jnp.int32), pltpu.SemaphoreType.DMA((2, 3))],
        bytes_accessed=8 * groups * lanes,
        limit=2 << 20,
    )(
        in_hbm(tracers.reshape(count * levels, length, 1, lanes)),
        in_hbm(velocity.reshape(2, levels, length, 1, lanes)),
        in_hbm(land_mask.reshape(levels, length, 1, lanes)),
    )
    first, last = first.reshape(2 * groups, lanes), last.reshape(2 * groups, lanes)
    before = lax.ppermute(last, "tx", up(tx))
    after = lax.ppermute(first, "tx", down(tx))

    held, flow, mask = in_vmem(tracers), in_vmem(velocity), in_vmem(land_mask)
    field = pltpu.VMEM(tracers.shape, f32)
    columns = pltpu.VMEM((levels, length, lanes), f32)
    stencils = pltpu.VMEM((5, levels, length, lanes), f32)
    partial, pack_first, pack_second, sideways = call(
        interior,
        (field, columns, columns, stencils),
        [VMEM] * 3,
        scratch=[stencils],
        flops=20 * cells,
        bytes_accessed=8 * cells,
        limit=2 << 20,
    )(held, flow, mask)
    partial = call(
        ecology,
        field,
        [VMEM] * 4 + [SMEM] * 6 + [VMEM],
        scratch=[
            pltpu.VMEM((8 * grazers, 16 * NPHY), jnp.bfloat16),
            pltpu.VMEM((8 * NPHY, 16 * grazers), jnp.bfloat16),
        ],
        flops=40 * cells,
        bytes_accessed=8 * cells,
        limit=2 << 20,
        input_output_aliases={10: 0},
    )(
        held,
        mask,
        in_vmem(sunlight),
        in_vmem(palatable),
        growth_max,
        half_sat,
        light_half,
        graze_max,
        graze_half,
        stoichiometry,
        partial,
    )
    swept, pack_first, pack_second, partial = call(
        border,
        (pltpu.VMEM((count, levels, 16, lanes), f32), columns, columns, field),
        [VMEM] * 5 + [ANY] * 3,
        out_specs=[VMEM] * 3 + [ANY],
        scratch=[stencils],
        flops=10 * cells,
        bytes_accessed=8 * cells,
        limit=2 << 20,
        input_output_aliases={5: 3, 6: 1, 7: 2},
    )(held, flow, mask, in_vmem(before), in_vmem(after), partial, pack_first, pack_second)
    pair = lambda n, odd: [p for i in range(odd, n, 2) for p in ((i, (i + 1) % n), ((i + 1) % n, i))]
    turns = (pair(ty, 0), pair(ty, 1)) if swaps(ty) else (up(ty), down(ty))
    from_first = lax.ppermute(pack_first, "ty", turns[0])
    from_second = lax.ppermute(pack_second, "ty", turns[1])
    partial, ready = call(
        border_across,
        (field, pltpu.VMEM((PREPARED, levels, length, lanes), f32)),
        [VMEM] * 7,
        flops=10 * cells,
        bytes_accessed=6 * cells,
        limit=2 << 20,
        input_output_aliases={6: 0},
    )(swept, flow, mask, sideways, pack_first, pack_second, partial)
    return call(
        finish,
        (field, jax.ShapeDtypeStruct(tracers.shape, f32)),
        [VMEM] * 4,
        out_specs=[VMEM, HBM],
        input_output_aliases={3: 0},
        scratch=[
            pltpu.VMEM((levels, length, lanes), f32),
            pltpu.VMEM((levels, length, lanes), f32),
            pltpu.SemaphoreType.DMA((count // 2,)),
        ],
        flops=4 * cells,
        bytes_accessed=8 * cells,
        limit=2 << 20,
    )(ready, in_vmem(from_first), in_vmem(from_second), partial)[1]


def solution(mesh):
    return jax.shard_map(
        shards,
        mesh=mesh,
        in_specs=(
            P("member", None, "tx", "ty"),
            P(None, None, "tx", "ty"),
            P(None, "tx", "ty"),
            P("tx", "ty"),
            P("member"),
            P("member", None),
            P("member"),
            P("member"),
            P("member"),
            P("member", None),
            P(),
        ),
        out_specs=P("member", None, "tx", "ty"),
        check_vma=False,
    )
```

```python
import jax
import jax.numpy as jnp
from jax import lax
from jax.experimental import pallas as pl
from jax.experimental.pallas import tpu as pltpu
from jax.sharding import PartitionSpec as P


NNUT = 4
NPHY = 26
DEPTH = 12

plankton_mortality = 0.05
grazer_mortality = 0.3
assimilation = 0.3
attenuation = 0.4

VMEM = pl.BlockSpec(memory_space=pltpu.VMEM)
SMEM = pl.BlockSpec(memory_space=pltpu.SMEM)
ANY = pl.BlockSpec(memory_space=pl.ANY)
HBM = pl.BlockSpec(memory_space=pltpu.HBM)


def in_vmem(array):
    return pltpu.with_memory_space_constraint(array, pltpu.VMEM)


def in_hbm(array):
    return pltpu.with_memory_space_constraint(array, pltpu.HBM)


def call(kernel, outs, specs, scratch=(), flops=0, bytes_accessed=0, limit=8 << 20, **more):
    return pl.pallas_call(
        kernel,
        out_shape=outs,
        in_specs=specs,
        scratch_shapes=list(scratch),
        cost_estimate=pl.CostEstimate(flops=flops, bytes_accessed=bytes_accessed, transcendentals=0),
        compiler_params=pltpu.CompilerParams(vmem_limit_bytes=limit),
        **more,
    )


class Deferred:
    def __init__(self, depth):
        self.depth, self.queue = depth, []

    def put(self, ref, index, value):
        self.queue.append((ref, index, value))
        if len(self.queue) > self.depth:
            self.pop()

    def pop(self):
        ref, index, value = self.queue.pop(0)
        ref[index] = value

    def flush(self):
        while self.queue:
            self.pop()


def diet_matrices(palatable, to_grazers, to_plants):
    f32, bf16 = jnp.float32, jnp.bfloat16
    grazers = palatable.shape[0]

    def picks(shape, dim, period):
        index = lax.broadcasted_iota(jnp.int32, shape, dim)
        index = jnp.where(index < period, index, index - period)
        other = lax.broadcasted_iota(jnp.int32, shape, 1 - dim)
        return jnp.where((index >> 3) == other, 1.0, 0.0).astype(bf16)

    def spread(left, middle, right, transposed):
        dims = (((1,), (1 if transposed else 0,)), ((), ()))
        part = lax.dot_general(left, middle, dims, preferred_element_type=f32).astype(bf16)
        whole = jnp.dot(part, right, preferred_element_type=f32)
        row = lax.broadcasted_iota(jnp.int32, whole.shape, 0) & 7
        col = lax.broadcasted_iota(jnp.int32, whole.shape, 1) & 7
        return jnp.where(row == col, whole, 0.0).astype(bf16)

    eats = palatable[...].astype(f32).astype(bf16)
    rows_z, rows_k = 8 * grazers, 8 * NPHY
    to_grazers[...] = spread(
        picks((rows_z, grazers), 0, rows_z), eats, picks((NPHY, 2 * rows_k), 1, rows_k), False
    )
    to_plants[...] = spread(
        picks((rows_k, NPHY), 0, rows_k), eats, picks((grazers, 2 * rows_z), 1, rows_z), True
    )


def pack_rows(tracers, velocity, mask, first, last, edge, sems):
    count, length = tracers.shape[0], tracers.shape[1]
    levels = mask.shape[0]
    forcing = pl.ds(count, levels)
    copies = []
    for side, (out, rows, row) in enumerate(
        ((first, pl.ds(0, 2), pl.ds(0, 1)), (last, pl.ds(length - 2, 2), pl.ds(length - 1, 1)))
    ):
        copies += [
            pltpu.make_async_copy(tracers.at[:, rows], out.at[pl.ds(0, count)], sems.at[side, 0]),
            pltpu.make_async_copy(
                velocity.at[0, :, row], out.at[forcing, pl.ds(0, 1)], sems.at[side, 1]
            ),
            pltpu.make_async_copy(mask.at[:, row], edge.at[side], sems.at[side, 2]),
        ]
    for copy in copies:
        copy.start()
    for out in (first, last):
        out[count + levels :] = jnp.zeros_like(out[count + levels :])
    for copy in copies:
        copy.wait()
    for side, out in enumerate((first, last)):
        out[forcing, pl.ds(1, 1)] = edge[side].astype(jnp.float32)


def ecology(
    tracers,
    mask,
    sunlight,
    palatable,
    growth_max,
    half_sat,
    light_half,
    graze_max,
    graze_half,
    stoichiometry,
    _,
    tendency,
    to_grazers,
    to_plants,
):
    count, levels, length, lanes = tracers.shape
    grazers = count - NNUT - NPHY
    f32, bf16 = jnp.float32, jnp.bfloat16
    plants = pl.ds(NNUT, NPHY)

    diet_matrices(palatable, to_grazers, to_plants)

    def split(values):
        wide = jnp.concatenate([v.reshape(-1, lanes) for v in values], axis=1)
        high = wide.astype(bf16)
        return jnp.concatenate([high, (wide - high.astype(f32)).astype(bf16)], axis=0)

    def entry(wide, n):
        part = wide[8 * n : 8 * n + 8]
        return jnp.concatenate([part[:, :lanes], part[:, lanes:]], axis=0)

    def level_step(level, carry):
        depth = jnp.exp(jnp.full((8, 128), -attenuation * (level + 0.5), f32))[0:1, 0:1]
        for start in range(0, length, 16):
            rows = pl.ds(start, 16)
            halves = (pl.ds(start, 8), pl.ds(start + 8, 8))
            available = jnp.dot(
                to_grazers[...],
                split([tracers[plants, level, half] for half in halves]),
                preferred_element_type=f32,
            )
            wet = mask[level, rows].astype(f32)
            recycled = jnp.zeros((16, lanes), f32)
            rates = []
            later = Deferred(DEPTH)

            def add(t, change):
                later.put(tendency, (t, level, rows), tendency[t, level, rows] + wet * change)

            for z in range(grazers):
                grazer = tracers[NNUT + NPHY + z, level, rows]
                prey = entry(available, z)
                rate = graze_max[z] * grazer / (graze_half[z] + prey)
                ingested = rate * prey
                loss = grazer_mortality * grazer * grazer
                add(NNUT + NPHY + z, assimilation * ingested - loss)
                recycled = recycled + (loss + (1.0 - assimilation) * ingested)
                rates.append(rate)
            pressure = jnp.dot(
                to_plants[...],
                split([jnp.concatenate([r[n : n + 8] for r in rates], axis=0) for n in (0, 8)]),
                preferred_element_type=f32,
            )
            darkness = 1.0 / (sunlight[rows] * depth)
            scarcity = [1.0 / tracers[j, level, rows] for j in range(NNUT)]
            for k in range(NPHY):
                plant = tracers[NNUT + k, level, rows]
                worst = half_sat[0, k] * scarcity[0]
                for j in range(1, NNUT):
                    worst = jnp.maximum(worst, half_sat[j, k] * scarcity[j])
                growth = (growth_max[k] * plant) / (
                    (1.0 + worst) * (1.0 + light_half[k] * darkness)
                )
                recycled = recycled + (plankton_mortality * plant - growth)
                add(NNUT + k, growth - plant * (entry(pressure, k) + plankton_mortality))
            for j in range(NNUT):
                add(j, stoichiometry[j] * recycled)
            later.flush()
        return carry

    for level in range(levels):
        level_step(level, 0)


def face_terms(u):
    up, down = jnp.maximum(u, 0.0), jnp.minimum(u, 0.0)
    return (
        up * (-1.0 / 6.0),
        up * (5.0 / 6.0) + down * (1.0 / 3.0),
        up * (1.0 / 3.0) + down * (5.0 / 6.0),
        down * (-1.0 / 6.0),
    )


def stencil(lower, upper):
    a0, b0, d0, e0 = face_terms(lower)
    a1, b1, d1, e1 = face_terms(upper)
    return a0, b0 - a1, 1.0 + (upper - lower) + d0 - b1, e0 - d1, -e1


def row_weights(velocity, mask, level, wet_before, wet_after, flow_after):
    length, lanes = mask.shape[1:]
    rows = lax.broadcasted_iota(jnp.int32, (length, lanes), 0)
    wet = mask[level].astype(jnp.float32)
    wet_up = jnp.where(rows == 0, wet_before, pltpu.roll(wet, 1, 0))
    lower = velocity[0, level] * (wet_up * wet)
    upper = jnp.where(
        rows == length - 1, flow_after * (wet * wet_after), pltpu.roll(lower, length - 1, 0)
    )
    return stencil(lower, upper)


def column_weights(velocity, mask, level, here):
    lanes = mask.shape[2]
    lane = lax.broadcasted_iota(jnp.int32, (8, lanes), 1)
    wet = mask[level, here].astype(jnp.float32)
    lower = jnp.where(lane == 0, 0.0, velocity[1, level, here] * wet * pltpu.roll(wet, 1, 1))
    upper = pltpu.roll(lower, lanes - 1, 1)
    wm2, wm1, w0, wp1, wp2 = stencil(lower, upper)
    return (
        jnp.where(lane < 2, 0.0, wm2),
        jnp.where(lane < 1, 0.0, wm1),
        w0,
        jnp.where(lane > lanes - 2, 0.0, wp1),
        jnp.where(lane > lanes - 3, 0.0, wp2),
    )


def sweep_across(centre, weights):
    wm2, wm1, w0, wp1, wp2 = weights
    lanes = centre.shape[1]
    return (
        w0 * centre
        + (wm1 * pltpu.roll(centre, 1, 1) + wm2 * pltpu.roll(centre, 2, 1))
        + (wp1 * pltpu.roll(centre, lanes - 1, 1) + wp2 * pltpu.roll(centre, lanes - 2, 1))
    )


def swaps(size):
    return size % 2 == 0


def first_is_right():
    size = lax.axis_size("ty")
    if not swaps(size):
        return True, True
    even = lax.axis_index("ty") % 2 == 0
    return even, jnp.logical_not(even)


def pick(choice, a, b):
    return (a if choice else b) if isinstance(choice, bool) else jnp.where(choice, a, b)


class Packer:
    def __init__(self, count, velocity, mask, level, here):
        wet = mask[level, here].astype(jnp.float32)
        lane = lax.broadcasted_iota(jnp.int32, wet.shape, 1)
        self.slot = lane // 2
        self.left = self.right = jnp.zeros_like(wet)
        self.add(count, jnp.where(lane < 2, velocity[1, level, here] * wet, wet))

    def add(self, t, value):
        turned = pltpu.roll(value, 2 * t + 2, 1)
        self.right = jnp.where(self.slot == t, turned, self.right)
        self.left = jnp.where(self.slot == t + 1, turned, self.left)


def interior(
    tracers, velocity, mask, partial, pack_first, pack_second, columns, swept, weights
):
    count, levels, length, lanes = tracers.shape
    zero = jnp.zeros((1, lanes), jnp.float32)
    for level in range(levels):
        for n, w in enumerate(row_weights(velocity, mask, level, zero, zero, zero)):
            weights[n, level] = w
        for block in range(length // 8):
            here = pl.ds(8 * block, 8)
            for n, w in enumerate(column_weights(velocity, mask, level, here)):
                columns[n, level, here] = w
    to_right, _ = first_is_right()
    blocks = length // 8 - 2

    def step(index, carry):
        level = index // blocks
        begin = 8 * (1 + index % blocks)
        here = pl.ds(begin, 8)
        wm2, wm1, w0, wp1, wp2 = [weights[n, level, here] for n in range(5)]
        sideways = [columns[n, level, here] for n in range(5)]
        packer = Packer(count, velocity, mask, level, here)
        later = Deferred(DEPTH)
        for t in range(count):
            at = lambda offset: tracers[t, level, pl.ds(begin + offset, 8)]
            value = w0 * at(0) + (wm1 * at(-1) + wm2 * at(-2)) + (wp1 * at(1) + wp2 * at(2))
            packer.add(t, value)
            later.put(partial, (t, level, here), sweep_across(value, sideways))
        later.flush()
        pack_first[level, here] = pick(to_right, packer.right, packer.left)
        pack_second[level, here] = pick(to_right, packer.left, packer.right)
        return carry

    def clear(level, carry):
        for t in range(count):
            partial[t, level, 0:8] = jnp.zeros((8, lanes), jnp.float32)
            partial[t, level, length - 8 : length] = jnp.zeros((8, lanes), jnp.float32)
        return carry

    lax.fori_loop(0, levels, clear, 0)
    for index in range(levels * blocks):
        step(index, 0)
    sweep_border_inside(tracers, weights, swept)


def edge_rows(weights, side):
    wm2, wm1, w0, wp1, wp2 = weights
    row = lax.broadcasted_iota(jnp.int32, w0.shape, 0)
    if side == 0:
        near, far = row < 1, row < 2
        inside = (jnp.where(far, 0.0, wm2), jnp.where(near, 0.0, wm1), w0, wp1, wp2)
        return inside, (jnp.where(far, wm2, 0.0), jnp.where(near, wm1, 0.0))
    near, far = row > 6, row > 5
    inside = (wm2, wm1, w0, jnp.where(near, 0.0, wp1), jnp.where(far, 0.0, wp2))
    return inside, (jnp.where(far, wp2, 0.0), jnp.where(near, wp1, 0.0))


def sweep_border_inside(tracers, weights, swept):
    count, levels, length, _ = tracers.shape
    for level in range(levels):
        for side, first in enumerate((0, length - 8)):
            here = pl.ds(first, 8)
            (wm2, wm1, w0, wp1, wp2), _ = edge_rows([weights[n, level, here] for n in range(5)], side)
            later = Deferred(DEPTH)
            for t in range(count):
                centre = tracers[t, level, here]

                def at(offset):
                    if (offset < 0) == (side == 0):
                        return pltpu.roll(centre, -offset % 8, 0)
                    return tracers[t, level, pl.ds(first + offset, 8)]

                value = w0 * centre + (wm1 * at(-1) + wm2 * at(-2)) + (wp1 * at(1) + wp2 * at(2))
                later.put(swept, (t, level, pl.ds(8 * side, 8)), value)
            later.flush()


def border(
    tracers,
    velocity,
    mask,
    before,
    after,
    _partial,
    _first,
    _second,
    _swept,
    swept,
    pack_first,
    pack_second,
    through,
):
    count, levels, length, lanes = tracers.shape
    zero = jnp.zeros((1, lanes), jnp.float32)
    to_right, _ = first_is_right()
    for level in range(levels):
        row = lambda ref, field: ref[pl.ds(2 * (count * levels + level) + field, 1)]
        opened = row_weights(velocity, mask, level, row(before, 1), row(after, 1), row(after, 0))
        closed = row_weights(velocity, mask, level, zero, zero, zero)
        for side, first in enumerate((0, length - 8)):
            here, there = pl.ds(first, 8), pl.ds(8 * side, 8)
            inside, (z2, z1) = edge_rows([w[first : first + 8] for w in opened], side)
            shut, _ = edge_rows([w[first : first + 8] for w in closed], side)
            own = inside[2] - shut[2]
            inward = inside[3] - shut[3] if side == 0 else inside[1] - shut[1]
            packer = Packer(count, velocity, mask, level, here)
            later = Deferred(DEPTH)
            for t in range(count):
                group = 2 * (t * levels + level)
                if side == 0:
                    beyond = z2 * before[pl.ds(group, 8)] + z1 * before[pl.ds(group + 1, 8)]
                elif group < 7:
                    outside = after[pl.ds(group, 8)]
                    beyond = z2 * pltpu.roll(outside, 6, 0) + z1 * pltpu.roll(outside, 7, 0)
                else:
                    beyond = z2 * after[pl.ds(group - 6, 8)] + z1 * after[pl.ds(group - 7, 8)]
                next_in = tracers[t, level, pl.ds(first + (1 if side == 0 else -1), 8)]
                value = (swept[t, level, there] + beyond) + (
                    own * tracers[t, level, here] + inward * next_in
                )
                later.put(swept, (t, level, there), value)
                packer.add(t, value)
            later.flush()
            pack_first[level, here] = pick(to_right, packer.right, packer.left)
            pack_second[level, here] = pick(to_right, packer.left, packer.right)


PREPARED = 8


def border_across(swept, velocity, mask, columns, my_first, my_second, _, partial, ready):
    count, levels, _, lanes = swept.shape
    length = mask.shape[1]
    place, size = lax.axis_index("ty"), lax.axis_size("ty")
    has_left = jnp.where(place > 0, 1.0, 0.0)
    has_right = jnp.where(place < size - 1, 1.0, 0.0)
    col = lambda value, n: jnp.broadcast_to(value[:, n : n + 1], value.shape)

    def step(index, carry):
        level, side = index // 2, index % 2
        here = pl.ds(side * (length - 8), 8)
        sideways = [columns[n, level, here] for n in range(5)]
        later = Deferred(DEPTH)
        for t in range(count):
            value = swept[t, level, pl.ds(8 * side, 8)]
            later.put(partial, (t, level, here), partial[t, level, here] + sweep_across(value, sideways))
        later.flush()
        return carry

    for index in range(2 * levels):
        step(index, 0)

    def prepare(level, carry):
        for block in range(length // 8):
            here = pl.ds(8 * block, 8)
            wet = mask[level, here].astype(jnp.float32)
            flow = velocity[1, level, here]
            opened = flow * wet * pltpu.roll(wet, 1, 1)
            to_right, _ = first_is_right()
            first, second = my_first[level, here], my_second[level, here]
            left, right = pick(to_right, second, first), pick(to_right, first, second)
            arrays = (
                col(flow * wet, 0) * has_left,
                col(wet, lanes - 1) * has_right,
                face_terms(col(opened, 1))[0] * has_left,
                face_terms(col(opened, lanes - 1))[3] * has_right,
                pltpu.roll(left, lanes - 2, 1),
                pltpu.roll(left, lanes - 3, 1),
                pltpu.roll(right, lanes - 2, 1),
                pltpu.roll(right, lanes - 1, 1),
            )
            for n, array in enumerate(arrays):
                ready[n, level, here] = array
        return carry

    for level in range(levels):
        prepare(level, 0)


def finish(ready, first, second, _, done, updated, even, odd, sems):
    count, levels, length, lanes = done.shape
    blocks = length // 8
    lane = lax.broadcasted_iota(jnp.int32, (8, lanes), 1)
    is_odd = lane % 2 == 1
    slot_odd = (lane // 2) % 2 == 1
    col = lambda value, n: jnp.broadcast_to(value[:, n : n + 1], value.shape)

    def level_step(level, carry):
        for block in range(blocks):
            here = pl.ds(8 * block, 8)
            open_low, open_high, a1, e127, s0, s1, s127, s126 = (
                ready[n, level, here] for n in range(PREPARED)
            )
            _, of_left = first_is_right()
            one, two = first[level, here], second[level, here]
            left = pick(of_left, one, two)
            right = pltpu.roll(pick(of_left, two, one), lanes - 4, 1)
            u0 = open_low * col(left, 2 * count + 1)
            u128 = open_high * col(right, 2 * count - 2)
            a0, b0, d0, e0 = face_terms(u0)
            a128, b128, d128, e128 = face_terms(u128)
            low = jnp.where(is_odd, a1, a0) * left + jnp.where(
                is_odd,
                0.0,
                (b0 - a1) * pltpu.roll(left, lanes - 1, 1) + ((d0 - u0) * s0 + e0 * s1),
            )
            high = jnp.where(
                is_odd,
                (e127 - d128) * pltpu.roll(right, 1, 1) + ((u128 - b128) * s127 - a128 * s126),
                0.0,
            ) - jnp.where(is_odd, e128, e127) * right
            even[level, here] = jnp.where(slot_odd, high, low)
            odd[level, here] = jnp.where(slot_odd, low, high)
        return carry

    for level in range(levels):
        level_step(level, 0)
    outer = (lane < 2) | (lane > lanes - 3)
    step = 4 if count % 4 == 0 else 2

    def copy(chunk):
        part = pl.ds(chunk * step, step)
        return pltpu.make_async_copy(done.at[part], updated.at[part], sems.at[chunk])

    def add(chunk, carry):
        start = chunk * step
        turns = [(lanes - 2 * (start + n)) % lanes for n in range(step)]
        later = Deferred(2 * DEPTH)
        for n in range(step):
            for level in range(levels):
                for block in range(blocks):
                    here = pl.ds(8 * block, 8)
                    edge = pltpu.roll((even, odd)[n % 2][level, here], turns[n], 1)
                    at = (start + n, level, here)
                    later.put(done, at, done[at] + jnp.where(outer, edge, 0.0))
        later.flush()
        copy(chunk).start()
        return carry

    def wait(chunk, carry):
        copy(chunk).wait()
        return carry

    for chunk in range(count // step):
        add(chunk, 0)
    lax.fori_loop(0, count // step, wait, 0)


def shards(
    tracers,
    velocity,
    land_mask,
    sunlight,
    growth_max,
    half_sat,
    light_half,
    graze_max,
    graze_half,
    palatable,
    stoichiometry,
):
    f32 = jnp.float32
    count, levels, length, lanes = tracers.shape
    tx, ty = lax.axis_size("tx"), lax.axis_size("ty")
    up = lambda n: [(i, (i + 1) % n) for i in range(n)]
    down = lambda n: [((i + 1) % n, i) for i in range(n)]
    cells = count * levels * length * lanes

    assert length % 16 == 0 and count % 2 == 0 and 2 * count + 4 <= lanes
    groups = -(-(count * levels + levels + 1) // 4) * 4
    row_message = pltpu.VMEM((groups, 2, 1, lanes), f32)
    grazers = count - NNUT - NPHY
    first, last = call(
        pack_rows,
        (row_message, row_message),
        [HBM, HBM, HBM],
        scratch=[pltpu.VMEM((2, levels, 1, 1, lanes), jnp.int32), pltpu.SemaphoreType.DMA((2, 3))],
        bytes_accessed=8 * groups * lanes,
        limit=2 << 20,
    )(
        in_hbm(tracers.reshape(count * levels, length, 1, lanes)),
        in_hbm(velocity.reshape(2, levels, length, 1, lanes)),
        in_hbm(land_mask.reshape(levels, length, 1, lanes)),
    )
    first, last = first.reshape(2 * groups, lanes), last.reshape(2 * groups, lanes)
    before = lax.ppermute(last, "tx", up(tx))
    after = lax.ppermute(first, "tx", down(tx))

    held, flow, mask = in_vmem(tracers), in_vmem(velocity), in_vmem(land_mask)
    field = pltpu.VMEM(tracers.shape, f32)
    columns = pltpu.VMEM((levels, length, lanes), f32)
    stencils = pltpu.VMEM((5, levels, length, lanes), f32)
    ends = pltpu.VMEM((count, levels, 16, lanes), f32)
    partial, pack_first, pack_second, sideways, swept = call(
        interior,
        (field, columns, columns, stencils, ends),
        [VMEM] * 3,
        scratch=[stencils],
        flops=20 * cells,
        bytes_accessed=8 * cells,
        limit=2 << 20,
    )(held, flow, mask)
    partial = call(
        ecology,
        field,
        [VMEM] * 4 + [SMEM] * 6 + [VMEM],
        scratch=[
            pltpu.VMEM((8 * grazers, 16 * NPHY), jnp.bfloat16),
            pltpu.VMEM((8 * NPHY, 16 * grazers), jnp.bfloat16),
        ],
        flops=40 * cells,
        bytes_accessed=8 * cells,
        limit=2 << 20,
        input_output_aliases={10: 0},
    )(
        held,
        mask,
        in_vmem(sunlight),
        in_vmem(palatable),
        growth_max,
        half_sat,
        light_half,
        graze_max,
        graze_half,
        stoichiometry,
        partial,
    )
    swept, pack_first, pack_second, partial = call(
        border,
        (ends, columns, columns, field),
        [VMEM] * 5 + [ANY] * 3 + [VMEM],
        out_specs=[VMEM] * 3 + [ANY],
        flops=10 * cells,
        bytes_accessed=8 * cells,
        limit=2 << 20,
        input_output_aliases={5: 3, 6: 1, 7: 2, 8: 0},
    )(held, flow, mask, in_vmem(before), in_vmem(after), partial, pack_first, pack_second, swept)
    pair = lambda n, odd: [p for i in range(odd, n, 2) for p in ((i, (i + 1) % n), ((i + 1) % n, i))]
    turns = (pair(ty, 0), pair(ty, 1)) if swaps(ty) else (up(ty), down(ty))
    from_first = lax.ppermute(pack_first, "ty", turns[0])
    from_second = lax.ppermute(pack_second, "ty", turns[1])
    partial, ready = call(
        border_across,
        (field, pltpu.VMEM((PREPARED, levels, length, lanes), f32)),
        [VMEM] * 7,
        flops=10 * cells,
        bytes_accessed=6 * cells,
        limit=2 << 20,
        input_output_aliases={6: 0},
    )(swept, flow, mask, sideways, pack_first, pack_second, partial)
    return call(
        finish,
        (field, jax.ShapeDtypeStruct(tracers.shape, f32)),
        [VMEM] * 4,
        out_specs=[VMEM, HBM],
        input_output_aliases={3: 0},
        scratch=[
            pltpu.VMEM((levels, length, lanes), f32),
            pltpu.VMEM((levels, length, lanes), f32),
            pltpu.SemaphoreType.DMA((count // 2,)),
        ],
        flops=4 * cells,
        bytes_accessed=8 * cells,
        limit=2 << 20,
    )(ready, in_vmem(from_first), in_vmem(from_second), partial)[1]


def solution(mesh):
    return jax.shard_map(
        shards,
        mesh=mesh,
        in_specs=(
            P("member", None, "tx", "ty"),
            P(None, None, "tx", "ty"),
            P(None, "tx", "ty"),
            P("tx", "ty"),
            P("member"),
            P("member", None),
            P("member"),
            P("member"),
            P("member"),
            P("member", None),
            P(),
        ),
        out_specs=P("member", None, "tx", "ty"),
        check_vma=False,
    )
```

```python
import jax
import jax.numpy as jnp
from jax import lax
from jax.experimental import pallas as pl
from jax.experimental.pallas import tpu as pltpu
from jax.sharding import PartitionSpec as P


NNUT = 4
NPHY = 26
DEPTH = 12

plankton_mortality = 0.05
grazer_mortality = 0.3
assimilation = 0.3
attenuation = 0.4

VMEM = pl.BlockSpec(memory_space=pltpu.VMEM)
SMEM = pl.BlockSpec(memory_space=pltpu.SMEM)
ANY = pl.BlockSpec(memory_space=pl.ANY)
HBM = pl.BlockSpec(memory_space=pltpu.HBM)


def in_vmem(array):
    return pltpu.with_memory_space_constraint(array, pltpu.VMEM)


def in_hbm(array):
    return pltpu.with_memory_space_constraint(array, pltpu.HBM)


def call(kernel, outs, specs, scratch=(), flops=0, bytes_accessed=0, limit=8 << 20, **more):
    return pl.pallas_call(
        kernel,
        out_shape=outs,
        in_specs=specs,
        scratch_shapes=list(scratch),
        cost_estimate=pl.CostEstimate(flops=flops, bytes_accessed=bytes_accessed, transcendentals=0),
        compiler_params=pltpu.CompilerParams(vmem_limit_bytes=limit),
        **more,
    )


class Deferred:
    def __init__(self, depth):
        self.depth, self.queue = depth, []

    def put(self, ref, index, value):
        self.queue.append((ref, index, value))
        if len(self.queue) > self.depth:
            self.pop()

    def pop(self):
        ref, index, value = self.queue.pop(0)
        ref[index] = value

    def flush(self):
        while self.queue:
            self.pop()


def diet_matrices(palatable, to_grazers, to_plants):
    f32, bf16 = jnp.float32, jnp.bfloat16
    grazers = palatable.shape[0]

    def picks(shape, dim, period):
        index = lax.broadcasted_iota(jnp.int32, shape, dim)
        index = jnp.where(index < period, index, index - period)
        other = lax.broadcasted_iota(jnp.int32, shape, 1 - dim)
        return jnp.where((index >> 3) == other, 1.0, 0.0).astype(bf16)

    def spread(left, middle, right, transposed):
        dims = (((1,), (1 if transposed else 0,)), ((), ()))
        part = lax.dot_general(left, middle, dims, preferred_element_type=f32).astype(bf16)
        whole = jnp.dot(part, right, preferred_element_type=f32)
        row = lax.broadcasted_iota(jnp.int32, whole.shape, 0) & 7
        col = lax.broadcasted_iota(jnp.int32, whole.shape, 1) & 7
        return jnp.where(row == col, whole, 0.0).astype(bf16)

    eats = palatable[...].astype(f32).astype(bf16)
    rows_z, rows_k = 8 * grazers, 8 * NPHY
    to_grazers[...] = spread(
        picks((rows_z, grazers), 0, rows_z), eats, picks((NPHY, 2 * rows_k), 1, rows_k), False
    )
    to_plants[...] = spread(
        picks((rows_k, NPHY), 0, rows_k), eats, picks((grazers, 2 * rows_z), 1, rows_z), True
    )


def pack_rows(tracers, velocity, mask, first, last, edge, sems):
    count, length = tracers.shape[0], tracers.shape[1]
    levels = mask.shape[0]
    forcing = pl.ds(count, levels)
    copies = []
    for side, (out, rows, row) in enumerate(
        ((first, pl.ds(0, 2), pl.ds(0, 1)), (last, pl.ds(length - 2, 2), pl.ds(length - 1, 1)))
    ):
        copies += [
            pltpu.make_async_copy(tracers.at[:, rows], out.at[pl.ds(0, count)], sems.at[side, 0]),
            pltpu.make_async_copy(
                velocity.at[0, :, row], out.at[forcing, pl.ds(0, 1)], sems.at[side, 1]
            ),
            pltpu.make_async_copy(mask.at[:, row], edge.at[side], sems.at[side, 2]),
        ]
    for copy in copies:
        copy.start()
    for out in (first, last):
        out[count + levels :] = jnp.zeros_like(out[count + levels :])
    for copy in copies:
        copy.wait()
    for side, out in enumerate((first, last)):
        out[forcing, pl.ds(1, 1)] = edge[side].astype(jnp.float32)


def ecology(
    tracers,
    mask,
    sunlight,
    palatable,
    growth_max,
    half_sat,
    light_half,
    graze_max,
    graze_half,
    stoichiometry,
    _,
    tendency,
    to_grazers,
    to_plants,
):
    count, levels, length, lanes = tracers.shape
    grazers = count - NNUT - NPHY
    f32, bf16 = jnp.float32, jnp.bfloat16
    plants = pl.ds(NNUT, NPHY)

    diet_matrices(palatable, to_grazers, to_plants)

    def split(values):
        wide = jnp.concatenate([v.reshape(-1, lanes) for v in values], axis=1)
        high = wide.astype(bf16)
        return jnp.concatenate([high, (wide - high.astype(f32)).astype(bf16)], axis=0)

    def entry(wide, n):
        part = wide[8 * n : 8 * n + 8]
        return jnp.concatenate([part[:, :lanes], part[:, lanes:]], axis=0)

    def level_step(level, carry):
        depth = jnp.exp(jnp.full((8, 128), -attenuation * (level + 0.5), f32))[0:1, 0:1]
        for start in range(0, length, 16):
            rows = pl.ds(start, 16)
            halves = (pl.ds(start, 8), pl.ds(start + 8, 8))
            available = jnp.dot(
                to_grazers[...],
                split([tracers[plants, level, half] for half in halves]),
                preferred_element_type=f32,
            )
            wet = mask[level, rows].astype(f32)
            recycled = jnp.zeros((16, lanes), f32)
            rates = []
            later = Deferred(DEPTH)

            def add(t, change):
                later.put(tendency, (t, level, rows), tendency[t, level, rows] + wet * change)

            for z in range(grazers):
                grazer = tracers[NNUT + NPHY + z, level, rows]
                prey = entry(available, z)
                rate = graze_max[z] * grazer / (graze_half[z] + prey)
                ingested = rate * prey
                loss = grazer_mortality * grazer * grazer
                add(NNUT + NPHY + z, assimilation * ingested - loss)
                recycled = recycled + (loss + (1.0 - assimilation) * ingested)
                rates.append(rate)
            pressure = jnp.dot(
                to_plants[...],
                split([jnp.concatenate([r[n : n + 8] for r in rates], axis=0) for n in (0, 8)]),
                preferred_element_type=f32,
            )
            darkness = 1.0 / (sunlight[rows] * depth)
            scarcity = [1.0 / tracers[j, level, rows] for j in range(NNUT)]
            for k in range(NPHY):
                plant = tracers[NNUT + k, level, rows]
                worst = half_sat[0, k] * scarcity[0]
                for j in range(1, NNUT):
                    worst = jnp.maximum(worst, half_sat[j, k] * scarcity[j])
                growth = (growth_max[k] * plant) / (
                    (1.0 + worst) * (1.0 + light_half[k] * darkness)
                )
                recycled = recycled + (plankton_mortality * plant - growth)
                add(NNUT + k, growth - plant * (entry(pressure, k) + plankton_mortality))
            for j in range(NNUT):
                add(j, stoichiometry[j] * recycled)
            later.flush()
        return carry

    for level in range(levels):
        level_step(level, 0)


def face_terms(u):
    up, down = jnp.maximum(u, 0.0), jnp.minimum(u, 0.0)
    return (
        up * (-1.0 / 6.0),
        up * (5.0 / 6.0) + down * (1.0 / 3.0),
        up * (1.0 / 3.0) + down * (5.0 / 6.0),
        down * (-1.0 / 6.0),
    )


def stencil(lower, upper):
    a0, b0, d0, e0 = face_terms(lower)
    a1, b1, d1, e1 = face_terms(upper)
    return a0, b0 - a1, 1.0 + (upper - lower) + d0 - b1, e0 - d1, -e1


def row_weights(velocity, mask, level, wet_before, wet_after, flow_after):
    length, lanes = mask.shape[1:]
    rows = lax.broadcasted_iota(jnp.int32, (length, lanes), 0)
    wet = mask[level].astype(jnp.float32)
    wet_up = jnp.where(rows == 0, wet_before, pltpu.roll(wet, 1, 0))
    lower = velocity[0, level] * (wet_up * wet)
    upper = jnp.where(
        rows == length - 1, flow_after * (wet * wet_after), pltpu.roll(lower, length - 1, 0)
    )
    return stencil(lower, upper)


def column_weights(velocity, mask, level, here):
    lanes = mask.shape[2]
    lane = lax.broadcasted_iota(jnp.int32, (8, lanes), 1)
    wet = mask[level, here].astype(jnp.float32)
    lower = jnp.where(lane == 0, 0.0, velocity[1, level, here] * wet * pltpu.roll(wet, 1, 1))
    upper = pltpu.roll(lower, lanes - 1, 1)
    wm2, wm1, w0, wp1, wp2 = stencil(lower, upper)
    return (
        jnp.where(lane < 2, 0.0, wm2),
        jnp.where(lane < 1, 0.0, wm1),
        w0,
        jnp.where(lane > lanes - 2, 0.0, wp1),
        jnp.where(lane > lanes - 3, 0.0, wp2),
    )


def sweep_across(centre, weights):
    wm2, wm1, w0, wp1, wp2 = weights
    lanes = centre.shape[1]
    return (
        w0 * centre
        + (wm1 * pltpu.roll(centre, 1, 1) + wm2 * pltpu.roll(centre, 2, 1))
        + (wp1 * pltpu.roll(centre, lanes - 1, 1) + wp2 * pltpu.roll(centre, lanes - 2, 1))
    )


def swaps(size):
    return size % 2 == 0


def first_is_right():
    size = lax.axis_size("ty")
    if not swaps(size):
        return True, True
    even = lax.axis_index("ty") % 2 == 0
    return even, jnp.logical_not(even)


def pick(choice, a, b):
    return (a if choice else b) if isinstance(choice, bool) else jnp.where(choice, a, b)


class Packer:
    def __init__(self, count, velocity, mask, level, here):
        wet = mask[level, here].astype(jnp.float32)
        lane = lax.broadcasted_iota(jnp.int32, wet.shape, 1)
        self.slot = lane // 2
        self.left = self.right = jnp.zeros_like(wet)
        self.add(count, jnp.where(lane < 2, velocity[1, level, here] * wet, wet))

    def add(self, t, value):
        turned = pltpu.roll(value, 2 * t + 2, 1)
        self.right = jnp.where(self.slot == t, turned, self.right)
        self.left = jnp.where(self.slot == t + 1, turned, self.left)


def interior(
    tracers, velocity, mask, partial, pack_first, pack_second, columns, swept, weights
):
    count, levels, length, lanes = tracers.shape
    zero = jnp.zeros((1, lanes), jnp.float32)
    for level in range(levels):
        for n, w in enumerate(row_weights(velocity, mask, level, zero, zero, zero)):
            weights[n, level] = w
        for block in range(length // 8):
            here = pl.ds(8 * block, 8)
            for n, w in enumerate(column_weights(velocity, mask, level, here)):
                columns[n, level, here] = w
    to_right, _ = first_is_right()
    blocks = length // 8 - 2

    def step(index, carry):
        level = index // blocks
        begin = 8 * (1 + index % blocks)
        here = pl.ds(begin, 8)
        wm2, wm1, w0, wp1, wp2 = [weights[n, level, here] for n in range(5)]
        sideways = [columns[n, level, here] for n in range(5)]
        packer = Packer(count, velocity, mask, level, here)
        later = Deferred(DEPTH)
        for t in range(count):
            at = lambda offset: tracers[t, level, pl.ds(begin + offset, 8)]
            value = w0 * at(0) + (wm1 * at(-1) + wm2 * at(-2)) + (wp1 * at(1) + wp2 * at(2))
            packer.add(t, value)
            later.put(partial, (t, level, here), sweep_across(value, sideways))
        later.flush()
        pack_first[level, here] = pick(to_right, packer.right, packer.left)
        pack_second[level, here] = pick(to_right, packer.left, packer.right)
        return carry

    def clear(level, carry):
        for t in range(count):
            partial[t, level, 0:8] = jnp.zeros((8, lanes), jnp.float32)
            partial[t, level, length - 8 : length] = jnp.zeros((8, lanes), jnp.float32)
        return carry

    lax.fori_loop(0, levels, clear, 0)
    for index in range(levels * blocks):
        step(index, 0)
    sweep_border_inside(tracers, weights, swept)


def edge_rows(weights, side):
    wm2, wm1, w0, wp1, wp2 = weights
    row = lax.broadcasted_iota(jnp.int32, w0.shape, 0)
    if side == 0:
        near, far = row < 1, row < 2
        inside = (jnp.where(far, 0.0, wm2), jnp.where(near, 0.0, wm1), w0, wp1, wp2)
        return inside, (jnp.where(far, wm2, 0.0), jnp.where(near, wm1, 0.0))
    near, far = row > 6, row > 5
    inside = (wm2, wm1, w0, jnp.where(near, 0.0, wp1), jnp.where(far, 0.0, wp2))
    return inside, (jnp.where(far, wp2, 0.0), jnp.where(near, wp1, 0.0))


def sweep_border_inside(tracers, weights, swept):
    count, levels, length, _ = tracers.shape
    for level in range(levels):
        for side, first in enumerate((0, length - 8)):
            here = pl.ds(first, 8)
            (wm2, wm1, w0, wp1, wp2), _ = edge_rows([weights[n, level, here] for n in range(5)], side)
            later = Deferred(DEPTH)
            for t in range(count):
                centre = tracers[t, level, here]

                def at(offset):
                    if (offset < 0) == (side == 0):
                        return pltpu.roll(centre, -offset % 8, 0)
                    return tracers[t, level, pl.ds(first + offset, 8)]

                value = w0 * centre + (wm1 * at(-1) + wm2 * at(-2)) + (wp1 * at(1) + wp2 * at(2))
                later.put(swept, (t, level, pl.ds(8 * side, 8)), value)
            later.flush()


def border(
    tracers,
    velocity,
    mask,
    before,
    after,
    _partial,
    _first,
    _second,
    _swept,
    swept,
    pack_first,
    pack_second,
    through,
):
    count, levels, length, lanes = tracers.shape
    zero = jnp.zeros((1, lanes), jnp.float32)
    to_right, _ = first_is_right()
    for level in range(levels):
        row = lambda ref, field: ref[pl.ds(2 * (count * levels + level) + field, 1)]
        opened = row_weights(velocity, mask, level, row(before, 1), row(after, 1), row(after, 0))
        closed = row_weights(velocity, mask, level, zero, zero, zero)
        for side, first in enumerate((0, length - 8)):
            here, there = pl.ds(first, 8), pl.ds(8 * side, 8)
            inside, (z2, z1) = edge_rows([w[first : first + 8] for w in opened], side)
            shut, _ = edge_rows([w[first : first + 8] for w in closed], side)
            own = inside[2] - shut[2]
            inward = inside[3] - shut[3] if side == 0 else inside[1] - shut[1]
            packer = Packer(count, velocity, mask, level, here)
            later = Deferred(DEPTH)
            for t in range(count):
                group = 2 * (t * levels + level)
                if side == 0:
                    beyond = z2 * before[pl.ds(group, 8)] + z1 * before[pl.ds(group + 1, 8)]
                elif group < 7:
                    outside = after[pl.ds(group, 8)]
                    beyond = z2 * pltpu.roll(outside, 6, 0) + z1 * pltpu.roll(outside, 7, 0)
                else:
                    beyond = z2 * after[pl.ds(group - 6, 8)] + z1 * after[pl.ds(group - 7, 8)]
                next_in = tracers[t, level, pl.ds(first + (1 if side == 0 else -1), 8)]
                value = (swept[t, level, there] + beyond) + (
                    own * tracers[t, level, here] + inward * next_in
                )
                later.put(swept, (t, level, there), value)
                packer.add(t, value)
            later.flush()
            pack_first[level, here] = pick(to_right, packer.right, packer.left)
            pack_second[level, here] = pick(to_right, packer.left, packer.right)


PREPARED = 8


def border_across(swept, velocity, mask, columns, my_first, my_second, _, partial, ready):
    count, levels, _, lanes = swept.shape
    length = mask.shape[1]
    place, size = lax.axis_index("ty"), lax.axis_size("ty")
    has_left = jnp.where(place > 0, 1.0, 0.0)
    has_right = jnp.where(place < size - 1, 1.0, 0.0)
    col = lambda value, n: jnp.broadcast_to(value[:, n : n + 1], value.shape)

    def step(index, carry):
        level, side = index // 2, index % 2
        here = pl.ds(side * (length - 8), 8)
        sideways = [columns[n, level, here] for n in range(5)]
        later = Deferred(DEPTH)
        for t in range(count):
            value = swept[t, level, pl.ds(8 * side, 8)]
            later.put(partial, (t, level, here), partial[t, level, here] + sweep_across(value, sideways))
        later.flush()
        return carry

    for index in range(2 * levels):
        step(index, 0)

    def prepare(level, carry):
        for block in range(length // 8):
            here = pl.ds(8 * block, 8)
            wet = mask[level, here].astype(jnp.float32)
            flow = velocity[1, level, here]
            opened = flow * wet * pltpu.roll(wet, 1, 1)
            to_right, _ = first_is_right()
            first, second = my_first[level, here], my_second[level, here]
            left, right = pick(to_right, second, first), pick(to_right, first, second)
            arrays = (
                col(flow * wet, 0) * has_left,
                col(wet, lanes - 1) * has_right,
                face_terms(col(opened, 1))[0] * has_left,
                face_terms(col(opened, lanes - 1))[3] * has_right,
                pltpu.roll(left, lanes - 2, 1),
                pltpu.roll(left, lanes - 3, 1),
                pltpu.roll(right, lanes - 2, 1),
                pltpu.roll(right, lanes - 1, 1),
            )
            for n, array in enumerate(arrays):
                ready[n, level, here] = array
        return carry

    for level in range(levels):
        prepare(level, 0)


def finish(ready, first, second, _, done, updated, even, odd, sems):
    count, levels, length, lanes = done.shape
    blocks = length // 8
    lane = lax.broadcasted_iota(jnp.int32, (8, lanes), 1)
    is_odd = lane % 2 == 1
    slot_odd = (lane // 2) % 2 == 1
    col = lambda value, n: jnp.broadcast_to(value[:, n : n + 1], value.shape)

    def level_step(level, carry):
        for block in range(blocks):
            here = pl.ds(8 * block, 8)
            open_low, open_high, a1, e127, s0, s1, s127, s126 = (
                ready[n, level, here] for n in range(PREPARED)
            )
            _, of_left = first_is_right()
            one, two = first[level, here], second[level, here]
            left = pick(of_left, one, two)
            right = pltpu.roll(pick(of_left, two, one), lanes - 4, 1)
            u0 = open_low * col(left, 2 * count + 1)
            u128 = open_high * col(right, 2 * count - 2)
            a0, b0, d0, e0 = face_terms(u0)
            a128, b128, d128, e128 = face_terms(u128)
            low = jnp.where(is_odd, a1, a0) * left + jnp.where(
                is_odd,
                0.0,
                (b0 - a1) * pltpu.roll(left, lanes - 1, 1) + ((d0 - u0) * s0 + e0 * s1),
            )
            high = jnp.where(
                is_odd,
                (e127 - d128) * pltpu.roll(right, 1, 1) + ((u128 - b128) * s127 - a128 * s126),
                0.0,
            ) - jnp.where(is_odd, e128, e127) * right
            even[level, here] = jnp.where(slot_odd, high, low)
            odd[level, here] = jnp.where(slot_odd, low, high)
        return carry

    outer = (lane < 2) | (lane > lanes - 3)
    step = max(n for n in (20, 10, 8, 4, 2) if count % n == 0)
    copies = []
    for level in range(levels):
        level_step(level, 0)
        for start in range(0, count, step):
            later = Deferred(4 * DEPTH)
            for t in range(start, start + step):
                for block in range(blocks):
                    here = pl.ds(8 * block, 8)
                    edge = pltpu.roll((even, odd)[t % 2][level, here], (lanes - 2 * t) % lanes, 1)
                    at = (t, level, here)
                    later.put(done, at, done[at] + jnp.where(outer, edge, 0.0))
            later.flush()
            part = (pl.ds(start, step), level)
            copies.append(pltpu.make_async_copy(done.at[part], updated.at[part], sems.at[len(copies)]))
            copies[-1].start()
    for copy in copies:
        copy.wait()


def shards(
    tracers,
    velocity,
    land_mask,
    sunlight,
    growth_max,
    half_sat,
    light_half,
    graze_max,
    graze_half,
    palatable,
    stoichiometry,
):
    f32 = jnp.float32
    count, levels, length, lanes = tracers.shape
    tx, ty = lax.axis_size("tx"), lax.axis_size("ty")
    up = lambda n: [(i, (i + 1) % n) for i in range(n)]
    down = lambda n: [((i + 1) % n, i) for i in range(n)]
    cells = count * levels * length * lanes

    assert length % 16 == 0 and count % 2 == 0 and 2 * count + 4 <= lanes
    groups = -(-(count * levels + levels + 1) // 4) * 4
    row_message = pltpu.VMEM((groups, 2, 1, lanes), f32)
    grazers = count - NNUT - NPHY
    first, last = call(
        pack_rows,
        (row_message, row_message),
        [HBM, HBM, HBM],
        scratch=[pltpu.VMEM((2, levels, 1, 1, lanes), jnp.int32), pltpu.SemaphoreType.DMA((2, 3))],
        bytes_accessed=8 * groups * lanes,
        limit=2 << 20,
    )(
        in_hbm(tracers.reshape(count * levels, length, 1, lanes)),
        in_hbm(velocity.reshape(2, levels, length, 1, lanes)),
        in_hbm(land_mask.reshape(levels, length, 1, lanes)),
    )
    first, last = first.reshape(2 * groups, lanes), last.reshape(2 * groups, lanes)
    before = lax.ppermute(last, "tx", up(tx))
    after = lax.ppermute(first, "tx", down(tx))

    held, flow, mask = in_vmem(tracers), in_vmem(velocity), in_vmem(land_mask)
    field = pltpu.VMEM(tracers.shape, f32)
    columns = pltpu.VMEM((levels, length, lanes), f32)
    stencils = pltpu.VMEM((5, levels, length, lanes), f32)
    ends = pltpu.VMEM((count, levels, 16, lanes), f32)
    partial, pack_first, pack_second, sideways, swept = call(
        interior,
        (field, columns, columns, stencils, ends),
        [VMEM] * 3,
        scratch=[stencils],
        flops=20 * cells,
        bytes_accessed=8 * cells,
        limit=2 << 20,
    )(held, flow, mask)
    partial = call(
        ecology,
        field,
        [VMEM] * 4 + [SMEM] * 6 + [VMEM],
        scratch=[
            pltpu.VMEM((8 * grazers, 16 * NPHY), jnp.bfloat16),
            pltpu.VMEM((8 * NPHY, 16 * grazers), jnp.bfloat16),
        ],
        flops=40 * cells,
        bytes_accessed=8 * cells,
        limit=2 << 20,
        input_output_aliases={10: 0},
    )(
        held,
        mask,
        in_vmem(sunlight),
        in_vmem(palatable),
        growth_max,
        half_sat,
        light_half,
        graze_max,
        graze_half,
        stoichiometry,
        partial,
    )
    swept, pack_first, pack_second, partial = call(
        border,
        (ends, columns, columns, field),
        [VMEM] * 5 + [ANY] * 3 + [VMEM],
        out_specs=[VMEM] * 3 + [ANY],
        flops=10 * cells,
        bytes_accessed=8 * cells,
        limit=2 << 20,
        input_output_aliases={5: 3, 6: 1, 7: 2, 8: 0},
    )(held, flow, mask, in_vmem(before), in_vmem(after), partial, pack_first, pack_second, swept)
    pair = lambda n, odd: [p for i in range(odd, n, 2) for p in ((i, (i + 1) % n), ((i + 1) % n, i))]
    turns = (pair(ty, 0), pair(ty, 1)) if swaps(ty) else (up(ty), down(ty))
    from_first = lax.ppermute(pack_first, "ty", turns[0])
    from_second = lax.ppermute(pack_second, "ty", turns[1])
    partial, ready = call(
        border_across,
        (field, pltpu.VMEM((PREPARED, levels, length, lanes), f32)),
        [VMEM] * 7,
        flops=10 * cells,
        bytes_accessed=6 * cells,
        limit=2 << 20,
        input_output_aliases={6: 0},
    )(swept, flow, mask, sideways, pack_first, pack_second, partial)
    return call(
        finish,
        (field, jax.ShapeDtypeStruct(tracers.shape, f32)),
        [VMEM] * 4,
        out_specs=[VMEM, HBM],
        input_output_aliases={3: 0},
        scratch=[
            pltpu.VMEM((levels, length, lanes), f32),
            pltpu.VMEM((levels, length, lanes), f32),
            pltpu.SemaphoreType.DMA((count // 2,)),
        ],
        flops=4 * cells,
        bytes_accessed=8 * cells,
        limit=2 << 20,
    )(ready, in_vmem(from_first), in_vmem(from_second), partial)[1]


def solution(mesh):
    return jax.shard_map(
        shards,
        mesh=mesh,
        in_specs=(
            P("member", None, "tx", "ty"),
            P(None, None, "tx", "ty"),
            P(None, "tx", "ty"),
            P("tx", "ty"),
            P("member"),
            P("member", None),
            P("member"),
            P("member"),
            P("member"),
            P("member", None),
            P(),
        ),
        out_specs=P("member", None, "tx", "ty"),
        check_vma=False,
    )
```
